32 devices in a mesh: dp: 16 (over z, x, core), head: 2 (over y).
Axes of the slice: x: 2, y: 2, z: 4, core: 2. Of those that a mesh axis runs over, the one named last changes fastest.
Arguments:
- patches: bfloat16 [32, 1024, 768], P('dp'), may hold values from -6 to 6
- keep_mask: int32 [32, 1024], P('dp'), may hold values 0 or 1
- counts: int32 [32], P('dp'), may hold values from 196 to 1024, as said below
- ln_gain: float32 [768], replicated, may hold values from 0.1 to 1.9
- w_in: bfloat16 [2, 768, 2688], P('head'), may hold values from -0.21875 to 0.21875
- q_gain: float32 [12, 64], P('head'), may hold values from 0.1 to 1.9
- k_gain: float32 [12, 64], P('head'), may hold values from 0.1 to 1.9
- w_out: bfloat16 [2, 1920, 768], P('head')
- d_out: bfloat16 [32, 1024, 768], P('dp'), may hold values from -6 to 6
Outputs:
- block_output: bfloat16 [32, 1024, 768], P('dp')
- d_in: bfloat16 [32, 1024, 768], P('dp')
- g_ln: float32 [768], P('dp')
- g_w_in: float32 [2, 768, 2688], P('head', 'dp')
- g_q: float32 [12, 64], P('head', 'dp')
- g_k: float32 [12, 64], P('head', 'dp')
- g_w_out: float32 [2, 1920, 768], P('head', None, 'dp')
The draws below stay inside these ranges and needn't reach their ends.
Inputs may be any that keep to these rules, and one draw needn't show every extreme that they name: `counts`: each count is 196, 576 or 1024; the first image's is 1024.
All inputs are finite; a program needn't handle non-finite values. No bound on the sum of `keep_mask` on one device may be relied on, other than what follows from the above.
Results may differ from the reference program's by a relative error of at most 0.0091.
Values sent between devices are 32-bit elements; how exact they have to be, the bound alone decides.
A program may use at most 256 MiB of HBM per device.

```python
import jax
import jax.numpy as jnp
from jax import lax

D = 768
HEADS = 12
HEAD_DIM = 64
FF = 3072
SLOTS = 1024
SEQS = 32
GROUPS = 2
HG = 6
GW = 2688
GO = 1920


def draw_counts(key, part):
    table = jnp.array([SLOTS * 49 // 256, SLOTS * 9 // 16, SLOTS], jnp.int32)
    picks = jax.random.randint(key, (SEQS,), 0, 3)
    picks = picks.at[0].set(2)
    return table[picks]


def draw_w_out(key, part):
    noise = jnp.clip(jax.random.normal(key, (GROUPS, GO, D), jnp.float32), -6.0, 6.0)
    row_ids = jnp.arange(GO)[None, :, None]
    factor = jnp.where(row_ids < D // GROUPS, 10.0 / D ** 0.5, 1.0 / FF ** 0.5)
    return (noise * factor).astype(jnp.bfloat16)


def plant(values, key, least, largest):
    longest = values.shape.index(max(values.shape))
    spots = []
    for shift in (0, 1):
        where = [jax.random.randint(jax.random.fold_in(key, axis), (), 0, length) for axis, length in enumerate(values.shape)]
        where[longest] = (where[longest] + shift) % values.shape[longest]
        spots.append(tuple(where))
    return values.at[spots[0]].set(least).at[spots[1]].set(largest)


def raised(drawn, own_key, source, target, shards_of, factor):
    def block_of(axis_at):
        return (jnp.arange(drawn.shape[axis_at]) // (drawn.shape[axis_at] // shards_of)).reshape((-1,) + (1,) * (drawn.ndim - 1 - axis_at))

    first = jax.random.permutation(own_key, shards_of)[block_of(target)]
    other_side = (block_of(target) + shards_of // 2) % shards_of
    return jnp.where((block_of(source) == first) | (block_of(source) == other_side), factor * drawn, drawn)


def levels(rng, extent, cuts, least, largest):
    loudness, own = 1.0, jax.random.fold_in(rng, 6)
    for dim, blocks in cuts:
        steps = jnp.exp(jax.random.uniform(jax.random.fold_in(own, dim), (blocks,), jnp.float32, least / len(cuts), largest / len(cuts)))
        loudness = loudness * jnp.repeat(steps, extent[dim] // blocks).reshape([-1 if axis == dim else 1 for axis in range(len(extent))])
    return loudness


def gaussian(key, dims, scale, most, pieces=(), kind=jnp.bfloat16):
    drawn = scale * jax.random.normal(key, dims, jnp.float32)
    if pieces:
        drawn = drawn * levels(key, dims, pieces, -0.22, 0.18)
    return jnp.clip(drawn, -most, most).astype(kind)


def noise_with(key, shape, deviation, most, shards, heavy, kind=jnp.bfloat16):
    values = deviation * jax.random.normal(key, shape, jnp.float32)
    if shards:
        values = values * levels(key, shape, shards, -0.22, 0.18)
    return jnp.clip(raised(values, jax.random.fold_in(key, 3), *heavy), -most, most).astype(kind)


def setup_inputs(seed: int = 0) -> dict:
    key_list = jax.random.split(jax.random.key(seed), 10)
    return {
        "patches": noise_with(key_list[0], (SEQS, SLOTS, D), 1.0, 6.0, ((0, 16),), (0, 2, 16, 2.0)),
        "keep_mask": plant((jax.random.randint(key_list[1], (SEQS, SLOTS), 0, 8) < 7).astype(jnp.int32), jax.random.fold_in(key_list[1], 1), 0, 1),
        "counts": draw_counts(jax.random.fold_in(key_list[9], 71), 0),
        "ln_gain": jnp.clip(1.0 + 0.18 * jax.random.normal(key_list[3], (D,), jnp.float32), 0.1, 1.9),
        "w_in": gaussian(key_list[4], (GROUPS, D, GW), D ** -0.5, 0.21875, ((0, 2),)),
        "q_gain": jnp.clip(1.0 + 0.18 * jax.random.normal(key_list[5], (HEADS, HEAD_DIM), jnp.float32), 0.1, 1.9),
        "k_gain": jnp.clip(1.0 + 0.18 * jax.random.normal(key_list[6], (HEADS, HEAD_DIM), jnp.float32), 0.1, 1.9),
        "w_out": draw_w_out(jax.random.fold_in(key_list[9], 71), 0),
        "d_out": noise_with(key_list[8], (SEQS, SLOTS, D), 1.0, 6.0, ((0, 16),), (0, 2, 16, 2.0)),
    }


@jax.custom_vjp
def low(v):
    return lax.optimization_barrier(v.astype(jnp.bfloat16)).astype(jnp.float32)

@jax.custom_vjp
def low_back(v):
    return v

def low_keep(v):
    return (low(v), None)

def low_pass(kept, grad):
    return (grad,)

def back_keep(v):
    return (v, None)

def back_low(kept, grad):
    return (low(grad),)
low.defvjp(low_keep, low_pass)
low_back.defvjp(back_keep, back_low)
epsilon = 1e-06

def norm_rows(v):
    centre = v - lax.optimization_barrier(jnp.mean(v, axis=-1, keepdims=True))
    spread = lax.optimization_barrier(jnp.mean(centre * centre, axis=-1, keepdims=True))
    return centre * lax.rsqrt(spread + epsilon)

def seq_forward(tokens, bias, ln_g, win, qg, kg, wout):
    highest = lax.Precision.HIGHEST
    inner = D // GROUPS
    normed = low(norm_rows(tokens) * ln_g)
    total = jnp.zeros((SLOTS, D), jnp.float32)
    for group in range(GROUPS):
        proj = low_back(jnp.dot(normed, win[group], precision=highest))
        query = proj[:, :inner].reshape(SLOTS, HG, HEAD_DIM)
        keys = proj[:, inner:2 * inner].reshape(SLOTS, HG, HEAD_DIM)
        values = low(proj[:, 2 * inner:3 * inner].reshape(SLOTS, HG, HEAD_DIM))
        hidden = low(jax.nn.gelu(proj[:, 3 * inner:], approximate=False))
        q_norm = low(norm_rows(query) * qg[group * HG:(group + 1) * HG])
        k_norm = low(norm_rows(keys) * kg[group * HG:(group + 1) * HG])
        scores = jnp.einsum('qhd,khd->hqk', q_norm, k_norm, precision=highest) * HEAD_DIM ** (-0.5)
        scores = low_back(scores + bias[None, None, :])
        top = lax.optimization_barrier(jnp.max(scores, axis=-1, keepdims=True))
        expo = jnp.exp(scores - top)
        probs = expo / lax.optimization_barrier(jnp.sum(expo, axis=-1, keepdims=True))
        attn = jnp.einsum('hqk,khd->qhd', low(probs), values, precision=highest)
        attn = low(low_back(attn)).reshape(SLOTS, inner)
        joined = jnp.concatenate([attn, hidden], axis=1)
        total = total + jnp.dot(joined, wout[group], precision=highest)
    return tokens + low_back(total)

def reference(patches, keep_mask, counts, ln_gain, w_in, q_gain, k_gain, w_out, d_out):
    slot_ids = jnp.arange(SLOTS, dtype=jnp.int32)
    valid = (slot_ids[None, :] < counts[:, None]) & ((keep_mask == 1) | (slot_ids[None, :] == 0))
    bias = jnp.where(valid, 0.0, -1000000000.0).astype(jnp.float32)

    def forward(tokens_all, ln_g, win, qg, kg, wout):

        def single(pair):
            return seq_forward(pair[0], pair[1], ln_g, win, qg, kg, wout)
        return lax.map(jax.checkpoint(single), (tokens_all, bias))
    result, backward = jax.vjp(forward, patches.astype(jnp.float32), ln_gain, w_in.astype(jnp.float32), q_gain, k_gain, w_out.astype(jnp.float32))
    grad_x, grad_ln, grad_in, grad_q, grad_k, grad_out = backward(d_out.astype(jnp.float32))
    return (result.astype(jnp.bfloat16), grad_x.astype(jnp.bfloat16), grad_ln, grad_in, grad_q, grad_k, grad_out)
```

```python
import functools
import math

import jax
import jax.numpy as jnp
from jax import lax
from jax.experimental import pallas as pl
from jax.experimental.pallas import tpu as pltpu
from jax.sharding import PartitionSpec as P

EPS = 1e-06
LOG2E = 1.4426950408889634
F32 = jnp.float32
BF16 = jnp.bfloat16
NT = (((1,), (1,)), ((), ()))
NN = (((1,), (0,)), ((), ()))


def mm(a, b, dims=NN):
    return lax.dot_general(a, b, dims, preferred_element_type=F32)


def gelu_parts(u):
    x = jnp.abs(u) * (1.0 / math.sqrt(2.0))
    d = 1.0 + 0.3275911 * x
    r = pl.reciprocal(d, approx=True)
    t = r * (2.0 - d * r)
    g = jnp.exp2(u * u * (-0.5 * LOG2E))
    poly = t * (0.254829592 + t * (-0.284496736 + t * (1.421413741 + t * (-1.453152027 + t * 1.061405429))))
    tail = 0.5 * poly * g
    cdf = jnp.where(u >= 0.0, 1.0 - tail, tail)
    return u * cdf, cdf + u * (g * (1.0 / math.sqrt(2.0 * math.pi)))


def head_norm(v, gain, heads, hdim):
    tokens = v.shape[-1]
    v = v.reshape(heads, hdim, tokens)
    centre = v - jnp.mean(v, axis=1, keepdims=True)
    r = lax.rsqrt(jnp.mean(centre * centre, axis=1, keepdims=True) + EPS)
    n = (centre * r).reshape(heads * hdim, tokens)
    return (n * gain).astype(BF16), r


def project_kernel(heads, hdim, x_ref, dz_ref, lng_ref, win_ref, wout_ref, qg_ref, kg_ref,
                   xnt_ref, dzt_ref, qt_ref, kt_ref, vt_ref, dot_ref, rq_ref, rk_ref, hid_ref, du_ref, wt_ref):
    inner = heads * hdim

    @pl.when(pl.program_id(0) == 0)
    def _():
        wt_ref[...] = win_ref[:, : 3 * inner].T

    x = x_ref[...].astype(F32)
    centre = x - jnp.mean(x, axis=-1, keepdims=True)
    r = lax.rsqrt(jnp.mean(centre * centre, axis=-1, keepdims=True) + EPS)
    xn = (centre * r * lng_ref[...]).astype(BF16)
    dz = dz_ref[...]
    xnt_ref[...] = xn.T
    dzt_ref[...] = dz.T
    qkv = mm(wt_ref[...], xn, NT)
    qn, rq = head_norm(qkv[:inner], qg_ref[...], heads, hdim)
    kn, rk = head_norm(qkv[inner : 2 * inner], kg_ref[...], heads, hdim)
    qt_ref[...] = qn
    kt_ref[...] = kn
    rq_ref[...] = rq
    rk_ref[...] = rk
    vt_ref[...] = qkv[2 * inner :].astype(BF16)
    dot_ref[...] = mm(wout_ref[:inner, :], dz, NT).astype(BF16)
    hidden = win_ref.shape[1] - 3 * inner
    step = 512
    for c in range(0, hidden, step):
        u = mm(xn, win_ref[:, 3 * inner + c : 3 * inner + c + step])
        dh = mm(dz, wout_ref[inner + c : inner + c + step, :], NT)
        h, slope = gelu_parts(u)
        hid_ref[:, c : c + step] = h.astype(BF16)
        du_ref[:, c : c + step] = (dh * slope).astype(BF16)


def project(x, dz, lng, win, wout, qg, kg, heads, hdim, tm=256):
    tokens, width = x.shape
    inner = heads * hdim
    gw = win.shape[1]
    hidden = gw - 3 * inner
    row = lambda n: pl.BlockSpec((tm, n), lambda i: (i, 0))
    col = lambda n: pl.BlockSpec((n, tm), lambda i: (0, i))
    whole = lambda a: pl.BlockSpec(a.shape, lambda i: (0,) * a.ndim, pipeline_mode=pl.Buffered(1))
    stat = pl.BlockSpec((heads, 1, tm), lambda i: (0, 0, i))
    sds = jax.ShapeDtypeStruct
    return pl.pallas_call(
        functools.partial(project_kernel, heads, hdim),
        grid=(tokens // tm,),
        in_specs=[row(width), row(width), whole(lng), whole(win), whole(wout), whole(qg), whole(kg)],
        out_specs=[col(width), col(width), col(inner), col(inner), col(inner), col(inner), stat, stat, row(hidden), row(hidden)],
        out_shape=[sds((width, tokens), BF16), sds((width, tokens), BF16)]
        + [sds((inner, tokens), BF16)] * 4
        + [sds((heads, 1, tokens), F32)] * 2
        + [sds((tokens, hidden), BF16)] * 2,
        scratch_shapes=[pltpu.VMEM((3 * inner, width), BF16)],
        compiler_params=pltpu.CompilerParams(vmem_limit_bytes=58 * 1024 * 1024),
        cost_estimate=pl.CostEstimate(
            flops=2 * tokens * width * (gw + wout.shape[0]), bytes_accessed=tokens * (width * 8 + hidden * 4 + inner * 8) + 4 * width * gw, transcendentals=2 * tokens * hidden
        ),
        name="project",
    )(x, dz, lng, win, wout, qg, kg)


def norm_back(dn, gain_col, unit, r):
    a = dn * gain_col
    m1 = jnp.mean(a, axis=0, keepdims=True)
    m2 = jnp.mean(a * unit, axis=0, keepdims=True)
    return r * (a - m1 - unit * m2)


def attend_kernel(hdim, bq, qt_ref, kt_ref, vt_ref, dot_ref, rq_ref, rk_ref, vrow_ref, qg_ref, kg_ref,
                  o_ref, dq_ref, dk_ref, dv_ref, gq_ref, gk_ref, dqt_s, dkt_s, dvt_s, ot_s):
    tokens = qt_ref.shape[1]
    vrow = vrow_ref[0]
    vrow_b = vrow.astype(BF16)
    scale = 0.125 if hdim == 64 else hdim ** (-0.5)
    for h in range(2):
        rows = slice(h * hdim, (h + 1) * hdim)
        kt = kt_ref[rows, :]
        vt = vt_ref[rows, :]
        kn = kt.T
        ktv = kt * vrow_b
        pad = jnp.zeros((16, tokens), BF16)
        sub = lax.broadcasted_iota(jnp.int32, (16, tokens), 0)
        va_sum = jnp.concatenate([vt * vrow_b, jnp.where(sub == 0, jnp.broadcast_to(vrow, (16, tokens)), 0.0).astype(BF16)], axis=0)
        va = jnp.concatenate([vt, jnp.where(sub < 2, 1.0, 0.0).astype(BF16)], axis=0).T
        dkt_s[rows, :] = jnp.zeros((hdim, tokens), F32)
        dvt_s[rows, :] = jnp.zeros((hdim, tokens), F32)

        def block(i, _):
            at = pl.ds(pl.multiple_of(i * bq, bq), bq)
            qb = qt_ref[rows, at]
            dob = dot_ref[rows, at]
            s = mm(kn, qb)
            e = jnp.exp2(s).astype(BF16)
            oa = mm(va_sum, e)
            linv = 1.0 / oa[hdim : hdim + 1, :]
            o = oa[:hdim, :] * linv
            ot_s[rows, at] = o.astype(BF16)
            dof = dob.astype(F32)
            delta = jnp.sum(dof * o, axis=0, keepdims=True) * linv
            hi = delta.astype(BF16)
            lo = (delta - hi.astype(F32)).astype(BF16)
            dos = (dof * linv).astype(BF16)
            sub16 = lax.broadcasted_iota(jnp.int32, (16, bq), 0)
            minus = jnp.where(sub16 == 0, -hi.astype(F32), jnp.where(sub16 == 1, -lo.astype(F32), 0.0)).astype(BF16)
            t = mm(va, jnp.concatenate([dos, minus], axis=0))
            ds = (e.astype(F32) * t).astype(BF16)
            dvt_s[rows, :] += mm(dos, e, NT)
            dkt_s[rows, :] += mm(qb, ds, NT)
            dqt_s[rows, at] = mm(ktv, ds)
            return 0

        lax.fori_loop(0, tokens // bq, block, 0)

    o_ref[...] = ot_s[...].T
    out = []
    for src, raw, r_ref, g_ref, grad_ref, mul, c in (
        (dqt_s, qt_ref, rq_ref, qg_ref, gq_ref, scale, scale * LOG2E),
        (dkt_s, kt_ref, rk_ref, kg_ref, gk_ref, 1.0 / LOG2E, 1.0),
    ):
        both = []
        for h in range(2):
            rows = slice(h * hdim, (h + 1) * hdim)
            g = g_ref[rows, :]
            unit = raw[rows, :].astype(F32) * (1.0 / (g * c))
            dn = src[rows, :] * mul
            if raw is kt_ref:
                dn = dn * vrow
            grad_ref[rows, :] = jnp.sum(dn * unit, axis=1, keepdims=True)
            both.append(norm_back(dn, g, unit, r_ref[h]).astype(BF16))
        out.append(jnp.concatenate(both, axis=0).T)
    dq_ref[...] = out[0]
    dk_ref[...] = out[1]
    dv_ref[...] = (dvt_s[...] * vrow).astype(BF16).T


def attend(qt, kt, vt, dot, rq, rk, vrow, qg, kg, heads, hdim, image, slots, bq=256):
    inner = heads * hdim
    pair = 2 * hdim
    sds = jax.ShapeDtypeStruct
    tcol = pl.BlockSpec((pair, slots), lambda p: (p, image))
    stat = pl.BlockSpec((2, 1, slots), lambda p: (p, 0, image))
    gain = pl.BlockSpec((pair, 1), lambda p: (p, 0))
    row = pl.BlockSpec((slots, pair), lambda p: (0, p))
    return pl.pallas_call(
        functools.partial(attend_kernel, hdim, bq),
        grid=(heads // 2,),
        in_specs=[tcol, tcol, tcol, tcol, stat, stat, pl.BlockSpec((1, 1, slots), lambda p: (image, 0, 0)), gain, gain],
        out_specs=[row, row, row, row, gain, gain],
        out_shape=[sds((slots, inner), BF16)] * 4 + [sds((inner, 1), F32)] * 2,
        scratch_shapes=[pltpu.VMEM((pair, slots), F32)] * 3 + [pltpu.VMEM((pair, slots), BF16)],
        compiler_params=pltpu.CompilerParams(vmem_limit_bytes=58 * 1024 * 1024),
        cost_estimate=pl.CostEstimate(flops=heads * 6 * 8 * slots * slots * hdim, bytes_accessed=16 * slots * inner, transcendentals=heads * slots * slots),
        name="attend",
    )(qt, kt, vt, dot, rq, rk, vrow, qg, kg)


def rows_kernel(transposed, a_ref, b_ref, wa_ref, wb_ref, out_ref):
    if transposed:
        out_ref[...] = mm(a_ref[...], wa_ref[...], NT) + mm(b_ref[...], wb_ref[...], NT)
    else:
        out_ref[...] = mm(a_ref[...], wa_ref[...]) + mm(b_ref[...], wb_ref[...])


def back_rows_kernel(inner, dq_ref, dk_ref, dv_ref, du_ref, w_ref, out_ref):
    out_ref[...] = (
        mm(dq_ref[...], w_ref[:, :inner], NT)
        + mm(dk_ref[...], w_ref[:, inner : 2 * inner], NT)
        + mm(dv_ref[...], w_ref[:, 2 * inner : 3 * inner], NT)
        + mm(du_ref[...], w_ref[:, 3 * inner :], NT)
    )


def back_rows(dq, dk, dv, du, win, image, tm=256):
    slots, inner = dq.shape
    width, gw = win.shape
    hidden = gw - 3 * inner
    steps = slots // tm
    row = pl.BlockSpec((tm, inner), lambda i: (i, 0))
    return pl.pallas_call(
        functools.partial(back_rows_kernel, inner),
        grid=(steps,),
        in_specs=[row, row, row, pl.BlockSpec((tm, hidden), lambda i: (image * steps + i, 0)), pl.BlockSpec(win.shape, lambda i: (0, 0), pipeline_mode=pl.Buffered(1))],
        out_specs=pl.BlockSpec((tm, width), lambda i: (i, 0)),
        out_shape=jax.ShapeDtypeStruct((slots, width), F32),
        compiler_params=pltpu.CompilerParams(vmem_limit_bytes=40 * 1024 * 1024),
        cost_estimate=pl.CostEstimate(flops=2 * slots * width * gw, bytes_accessed=slots * (2 * gw + 4 * width) + 2 * width * gw, transcendentals=0),
        name="back_rows",
    )(dq, dk, dv, du, win)


def out_rows_kernel(inner, o_ref, hid_ref, w_ref, out_ref):
    out_ref[...] = mm(o_ref[...], w_ref[:inner, :]) + mm(hid_ref[...], w_ref[inner:, :])


def out_rows(o, hid, wout, image, tm=256):
    slots, inner = o.shape
    go, width = wout.shape
    steps = slots // tm
    return pl.pallas_call(
        functools.partial(out_rows_kernel, inner),
        grid=(steps,),
        in_specs=[pl.BlockSpec((tm, inner), lambda i: (i, 0)), pl.BlockSpec((tm, go - inner), lambda i: (image * steps + i, 0)), pl.BlockSpec(wout.shape, lambda i: (0, 0), pipeline_mode=pl.Buffered(1))],
        out_specs=pl.BlockSpec((tm, width), lambda i: (i, 0)),
        out_shape=jax.ShapeDtypeStruct((slots, width), F32),
        compiler_params=pltpu.CompilerParams(vmem_limit_bytes=40 * 1024 * 1024),
        cost_estimate=pl.CostEstimate(flops=2 * slots * width * go, bytes_accessed=slots * (2 * go + 4 * width) + 2 * width * go, transcendentals=0),
        name="out_rows",
    )(o, hid, wout)


def per_device(patches, keep_mask, counts, ln_gain, w_in, q_gain, k_gain, w_out, d_out):
    seqs, slots, width = patches.shape
    heads, hdim = q_gain.shape
    inner = heads * hdim
    swap = [(0, 1), (1, 0)]
    scale = hdim ** (-0.5)
    win, wout = w_in[0], w_out[0]
    x = patches.reshape(seqs * slots, width)
    dz = d_out.reshape(seqs * slots, width)
    slot_ids = jnp.arange(slots, dtype=jnp.int32)
    valid = (slot_ids[None, :] < counts[:, None]) & ((keep_mask == 1) | (slot_ids[None, :] == 0))
    vrow = valid.astype(F32).reshape(seqs, 1, slots)
    qg = q_gain.reshape(inner, 1)
    kg = k_gain.reshape(inner, 1)
    xnt, dzt, qt, kt, vt, dot, rq, rk, hid, du = project(x, dz, ln_gain.reshape(1, width), win, wout, qg * (scale * LOG2E), kg, heads, hdim)
    outs, grads_in = [], []
    os, dqs, gqs, gks = [], [], [], []
    for s in range(seqs):
        o, dq, dk, dv, gq, gk = attend(qt, kt, vt, dot, rq, rk, vrow, qg, kg, heads, hdim, s, slots)
        dxn = back_rows(dq, dk, dv, du, win, s)
        grads_in.append((dxn, lax.ppermute(dxn, "head", swap)))
        z = out_rows(o, hid, wout, s)
        outs.append((z, lax.ppermute(z, "head", swap)))
        os.append(o)
        dqs.append(jnp.concatenate([dq, dk, dv], axis=1))
        gqs.append(gq)
        gks.append(gk)
    o = jnp.concatenate(os, axis=0)
    dqkv = jnp.concatenate(dqs, axis=0)
    d = lambda a, b: jnp.dot(a, b, preferred_element_type=F32)
    early = jnp.concatenate([d(dzt, hid), d(xnt, du)], axis=1)
    late = jnp.concatenate([d(dzt, o), d(xnt, dqkv)], axis=1)
    rs = lambda v: lax.psum_scatter(v, "dp", scatter_dimension=0, tiled=True)
    early = rs(early)
    late = rs(late)
    hidden = hid.shape[1]
    g_w_out = jnp.concatenate([late[:, :inner], early[:, :hidden]], axis=1).T[None]
    g_w_in = jnp.concatenate([late[:, inner:], early[:, hidden:]], axis=1)[None]
    block_output = jnp.stack([(patches[s].astype(F32) + outs[s][0] + outs[s][1]).astype(BF16) for s in range(seqs)])
    d_in, ln_term = [], jnp.zeros((width,), F32)
    for s in range(seqs):
        g = grads_in[s][0] + grads_in[s][1]
        xs = patches[s].astype(F32)
        centre = xs - jnp.mean(xs, axis=-1, keepdims=True)
        r = lax.rsqrt(jnp.mean(centre * centre, axis=-1, keepdims=True) + EPS)
        n = centre * r
        a = g * ln_gain
        back = r * (a - jnp.mean(a, axis=-1, keepdims=True) - n * jnp.mean(a * n, axis=-1, keepdims=True))
        d_in.append((d_out[s].astype(F32) + back).astype(BF16))
        ln_term = ln_term + jnp.sum(g * n, axis=0)
    d_in = jnp.stack(d_in)
    g_q = sum(gqs).reshape(heads, hdim)
    g_k = sum(gks).reshape(heads, hdim)
    return (
        block_output,
        d_in,
        rs(ln_term),
        g_w_in,
        lax.psum_scatter(g_q, "dp", scatter_dimension=1, tiled=True),
        lax.psum_scatter(g_k, "dp", scatter_dimension=1, tiled=True),
        g_w_out,
    )


def solution(mesh):
    placed = (
        P("dp", None, None),
        P("dp", None),
        P("dp"),
        P(),
        P("head", None, None),
        P("head", None),
        P("head", None),
        P("head", None, None),
        P("dp", None, None),
    )
    return jax.shard_map(
        per_device,
        mesh=mesh,
        in_specs=placed,
        out_specs=(
            P("dp", None, None),
            P("dp", None, None),
            P("dp"),
            P("head", "dp", None),
            P("head", "dp"),
            P("head", "dp"),
            P("head", None, "dp"),
        ),
        check_vma=False,
    )
```

```python
import functools
import math

import jax
import jax.numpy as jnp
from jax import lax
from jax.experimental import pallas as pl
from jax.experimental.pallas import tpu as pltpu
from jax.sharding import PartitionSpec as P

EPS = 1e-06
LOG2E = 1.4426950408889634
F32 = jnp.float32
BF16 = jnp.bfloat16
VMEM = 67000000
NT = (((1,), (1,)), ((), ()))
NN = (((1,), (0,)), ((), ()))


def cost(flops, bytes_accessed, transcendentals):
    return pl.CostEstimate(flops=flops, bytes_accessed=bytes_accessed, transcendentals=transcendentals)


def mm(a, b, dims=NN):
    return lax.dot_general(a, b, dims, preferred_element_type=F32)


def gelu_parts(u):
    cdf = 0.5 + 0.5 * lax.erf(u * math.sqrt(0.5))
    return u * cdf, cdf + u * (jnp.exp2(u * u * (-0.5 * LOG2E)) * (1.0 / math.sqrt(2.0 * math.pi)))


def head_norm(v, gain, heads, hdim):
    tokens = v.shape[-1]
    v = v.reshape(heads, hdim, tokens)
    centre = v - jnp.mean(v, axis=1, keepdims=True)
    r = lax.rsqrt(jnp.mean(centre * centre, axis=1, keepdims=True) + EPS)
    n = (centre * r).reshape(heads * hdim, tokens)
    return (n * gain).astype(BF16), r


def project_kernel(heads, hdim, x_ref, dz_ref, lng_ref, win_ref, wout_ref, qg_ref, kg_ref,
                   xnt_ref, dzt_ref, qt_ref, kt_ref, vt_ref, dot_ref, rq_ref, rk_ref, hid_ref, du_ref, wt_ref):
    inner = heads * hdim

    @pl.when(pl.program_id(0) == 0)
    def _():
        wt_ref[...] = win_ref[:, : 3 * inner].T

    x = x_ref[...].astype(F32)
    centre = x - jnp.mean(x, axis=-1, keepdims=True)
    r = lax.rsqrt(jnp.mean(centre * centre, axis=-1, keepdims=True) + EPS)
    xn = (centre * r * lng_ref[...]).astype(BF16)
    dz = dz_ref[...]
    xnt_ref[...] = xn.T
    dzt_ref[...] = dz.T
    qkv = mm(wt_ref[...], xn, NT)
    qn, rq = head_norm(qkv[:inner], qg_ref[...], heads, hdim)
    kn, rk = head_norm(qkv[inner : 2 * inner], kg_ref[...], heads, hdim)
    qt_ref[...] = qn
    kt_ref[...] = kn
    rq_ref[...] = rq
    rk_ref[...] = rk
    vt_ref[...] = qkv[2 * inner :].astype(BF16)
    dot_ref[...] = mm(wout_ref[:inner, :], dz, NT).astype(BF16)
    hidden = win_ref.shape[1] - 3 * inner
    step = 512
    for c in range(0, hidden, step):
        u = mm(xn, win_ref[:, 3 * inner + c : 3 * inner + c + step])
        dh = mm(dz, wout_ref[inner + c : inner + c + step, :], NT)
        h, slope = gelu_parts(u)
        hid_ref[:, c : c + step] = h.astype(BF16)
        du_ref[:, c : c + step] = (dh * slope).astype(BF16)


def project(x, dz, lng, win, wout, qg, kg, heads, hdim, image, slots, tm=256):
    width = x.shape[1]
    inner = heads * hdim
    gw = win.shape[1]
    hidden = gw - 3 * inner
    steps = slots // tm
    given = pl.BlockSpec((tm, width), lambda i: (image * steps + i, 0))
    row = lambda n: pl.BlockSpec((tm, n), lambda i: (i, 0))
    col = lambda n: pl.BlockSpec((n, tm), lambda i: (0, i))
    whole = lambda a: pl.BlockSpec(a.shape, lambda i: (0,) * a.ndim, pipeline_mode=pl.Buffered(1))
    stat = pl.BlockSpec((heads, 1, tm), lambda i: (0, 0, i))
    sds = jax.ShapeDtypeStruct
    return pl.pallas_call(
        functools.partial(project_kernel, heads, hdim),
        grid=(steps,),
        in_specs=[given, given, whole(lng), whole(win), whole(wout), whole(qg), whole(kg)],
        out_specs=[col(width), col(width), col(inner), col(inner), col(inner), col(inner), stat, stat, row(hidden), row(hidden)],
        out_shape=[sds((width, slots), BF16)] * 2
        + [sds((inner, slots), BF16)] * 4
        + [sds((heads, 1, slots), F32)] * 2
        + [sds((slots, hidden), BF16)] * 2,
        scratch_shapes=[pltpu.VMEM((3 * inner, width), BF16)],
        compiler_params=pltpu.CompilerParams(vmem_limit_bytes=VMEM),
        cost_estimate=cost(
            flops=2 * slots * width * (gw + wout.shape[0]), bytes_accessed=slots * (width * 8 + hidden * 4 + inner * 8) + 4 * width * gw, transcendentals=2 * slots * hidden
        ),
        name="project",
    )(x, dz, lng, win, wout, qg, kg)


def attend_kernel(hdim, bq, nh, qt_ref, kt_ref, vt_ref, dot_ref, rq_ref, rk_ref, vrow_ref, qg_ref, kg_ref,
                  o_ref, dq_ref, dk_ref, dv_ref, gq_ref, gk_ref, dqt_s, dkt_s, dvt_s, ot_s, kn_s, ktv_s, vs_s, va_s):
    tokens = qt_ref.shape[1]
    vrow = vrow_ref[0]
    vrow_b = vrow.astype(BF16)
    scale = hdim ** (-0.5)
    sub = lax.broadcasted_iota(jnp.int32, (16, tokens), 0)
    ones_row = jnp.where(sub == 0, jnp.broadcast_to(vrow, (16, tokens)), 0.0).astype(BF16)
    minus_row = jnp.where(sub < 2, 1.0, 0.0).astype(BF16)
    ktv_s[...] = kt_ref[...] * vrow_b
    for h in range(nh):
        rows = slice(h * hdim, (h + 1) * hdim)
        vt = vt_ref[rows, :]
        kn_s[h] = kt_ref[rows, :].T
        vs_s[h, :hdim, :] = vt * vrow_b
        vs_s[h, hdim:, :] = ones_row
        va_s[h] = jnp.concatenate([vt, minus_row], axis=0).T
    dkt_s[...] = jnp.zeros_like(dkt_s)
    dvt_s[...] = jnp.zeros_like(dvt_s)
    sub16 = lax.broadcasted_iota(jnp.int32, (16, bq), 0)

    def first(h, i):
        rows = slice(h * hdim, (h + 1) * hdim)
        at = pl.ds(pl.multiple_of(i * bq, bq), bq)
        return jnp.exp2(mm(kn_s[h], qt_ref[rows, at])).astype(BF16)

    def second(h, i, e):
        rows = slice(h * hdim, (h + 1) * hdim)
        at = pl.ds(pl.multiple_of(i * bq, bq), bq)
        qb = qt_ref[rows, at]
        dob = dot_ref[rows, at]
        oa = mm(vs_s[h], e)
        linv = 1.0 / oa[hdim : hdim + 1, :]
        o = oa[:hdim, :] * linv
        ot_s[rows, at] = o.astype(BF16)
        dof = dob.astype(F32)
        delta = jnp.sum(dof * o, axis=0, keepdims=True) * linv
        hi = delta.astype(BF16)
        lo = (delta - hi.astype(F32)).astype(BF16)
        dos = (dof * linv).astype(BF16)
        minus = jnp.where(sub16 == 0, -hi.astype(F32), jnp.where(sub16 == 1, -lo.astype(F32), 0.0)).astype(BF16)
        t = mm(va_s[h], jnp.concatenate([dos, minus], axis=0))
        ds = (e.astype(F32) * t).astype(BF16)
        dvt_s[rows, :] += mm(dos, e, NT)
        dkt_s[rows, :] += mm(qb, ds, NT)
        dqt_s[rows, at] = mm(ktv_s[rows, :], ds)

    def block(i, _):
        es = [first(h, i) for h in range(nh)]
        for h in range(nh):
            second(h, i, es[h])
        return 0

    lax.fori_loop(0, tokens // bq, block, 0, unroll=True)

    for p in range(nh // 2):
        prow = slice(p * 2 * hdim, (p + 1) * 2 * hdim)
        o_ref[:, prow] = ot_s[prow, :].T
        dv_ref[:, prow] = (dvt_s[prow, :] * vrow).astype(BF16).T
        for src, raw, r_ref, g_ref, grad_ref, dst, mul, c in (
            (dqt_s, qt_ref, rq_ref, qg_ref, gq_ref, dq_ref, scale, scale * LOG2E),
            (dkt_s, kt_ref, rk_ref, kg_ref, gk_ref, dk_ref, 1.0 / LOG2E, 1.0),
        ):
            both = []
            for h in (2 * p, 2 * p + 1):
                rows = slice(h * hdim, (h + 1) * hdim)
                g = g_ref[rows, :]
                inv = 1.0 / (g * c)
                d = src[rows, :]
                if raw is kt_ref:
                    d = d * vrow
                x = raw[rows, :].astype(F32)
                prod = d * x
                grad_ref[rows, :] = jnp.sum(prod, axis=1, keepdims=True) * (inv * mul)
                a = d * (g * mul)
                m1 = jnp.mean(a, axis=0, keepdims=True)
                m2 = jnp.mean(prod, axis=0, keepdims=True) * (mul / c)
                both.append((r_ref[h] * (a - m1 - (x * inv) * m2)).astype(BF16))
            dst[:, prow] = jnp.concatenate(both, axis=0).T

def attend(qt, kt, vt, dot, rq, rk, vrow, qg, kg, heads, hdim, slots, bq=256, nh=2):
    inner = heads * hdim
    w = nh * hdim
    sds = jax.ShapeDtypeStruct
    tcol = pl.BlockSpec((w, slots), lambda p: (p, 0))
    stat = pl.BlockSpec((nh, 1, slots), lambda p: (p, 0, 0))
    gain = pl.BlockSpec((w, 1), lambda p: (p, 0))
    row = pl.BlockSpec((slots, w), lambda p: (0, p))
    return pl.pallas_call(
        functools.partial(attend_kernel, hdim, bq, nh),
        grid=(heads // nh,),
        in_specs=[tcol, tcol, tcol, tcol, stat, stat, pl.BlockSpec((1, 1, slots), lambda p: (0, 0, 0)), gain, gain],
        out_specs=[row, row, row, row, gain, gain],
        out_shape=[sds((slots, inner), BF16)] * 4 + [sds((inner, 1), F32)] * 2,
        scratch_shapes=[pltpu.VMEM((w, slots), F32)] * 3 + [pltpu.VMEM((w, slots), BF16),
            pltpu.VMEM((nh, slots, hdim), BF16), pltpu.VMEM((w, slots), BF16), pltpu.VMEM((nh, hdim + 16, slots), BF16), pltpu.VMEM((nh, slots, hdim + 16), BF16)],
        compiler_params=pltpu.CompilerParams(vmem_limit_bytes=VMEM),
        cost_estimate=cost(flops=heads * 6 * 8 * slots * slots * hdim, bytes_accessed=16 * slots * inner, transcendentals=heads * slots * slots),
        name="attend",
    )(qt, kt, vt, dot, rq, rk, vrow, qg, kg)

def layer_norm(x_ref, lng_ref):
    x = x_ref[...].astype(F32)
    centre = x - jnp.mean(x, axis=-1, keepdims=True)
    r = lax.rsqrt(jnp.mean(centre * centre, axis=-1, keepdims=True) + EPS)
    return (centre * r * lng_ref[...]).astype(BF16)


def back_rows_kernel(inner, cuts, tm, dq_ref, dk_ref, dv_ref, du_ref, w_ref, *outs):
    g = (
        mm(dq_ref[...], w_ref[:, :inner], NT)
        + mm(dk_ref[...], w_ref[:, inner : 2 * inner], NT)
        + mm(dv_ref[...], w_ref[:, 2 * inner : 3 * inner], NT)
        + mm(du_ref[...], w_ref[:, 3 * inner :], NT)
    )
    step = pl.program_id(0)
    for k, out in enumerate(outs):
        low, high = cuts[k] // tm, cuts[k + 1] // tm
        if high - low == 1:

            @pl.when(step == low)
            def _(out=out):
                out[...] = g
        else:

            @pl.when((step >= low) & (step < high))
            def _(out=out, low=low):
                out[pl.ds(pl.multiple_of((step - low) * tm, tm), tm), :] = g


def back_rows(dq, dk, dv, du, win, cuts, tm=256):
    slots, inner = dq.shape
    width, gw = win.shape
    hidden = gw - 3 * inner
    steps = slots // tm
    row = lambda n: pl.BlockSpec((tm, n), lambda i: (i, 0))
    parts = [b - a for a, b in zip(cuts, cuts[1:])]
    return pl.pallas_call(
        functools.partial(back_rows_kernel, inner, cuts, tm),
        grid=(steps,),
        in_specs=[row(inner), row(inner), row(inner), row(hidden), pl.BlockSpec(win.shape, lambda i: (0, 0), pipeline_mode=pl.Buffered(1))],
        out_specs=[pl.BlockSpec((n, width), lambda i: (0, 0)) for n in parts],
        out_shape=[jax.ShapeDtypeStruct((n, width), F32) for n in parts],
        compiler_params=pltpu.CompilerParams(vmem_limit_bytes=VMEM),
        cost_estimate=cost(2 * slots * width * gw, slots * (2 * gw + 4 * width) + 2 * width * gw, 0),
        name="back_rows",
    )(dq, dk, dv, du, win)


def unpack_kernel(pieces, halved, me_ref, *refs):
    parts, (out_ref, stage, sem) = refs[:-3], refs[-3:]
    step = pl.program_id(0)

    def copies(i):
        slot = lax.rem(i, 2)
        for k in range(pieces):
            src = parts[k : k + 1] if k < pieces - halved else parts[pieces - halved + 2 * (k - pieces + halved) :][:2]

            @pl.when(jnp.bitwise_xor(i, me_ref[0]) == k)
            def _(src=src):
                rows = stage.shape[1] // len(src)
                for j, ref in enumerate(src):
                    pltpu.make_async_copy(ref, stage.at[slot, pl.ds(j * rows, rows)], sem.at[slot]).start()

    @pl.when(step == 0)
    def _():
        copies(step)

    @pl.when(step + 1 < pieces)
    def _():
        copies(step + 1)

    slot = lax.rem(step, 2)
    pltpu.make_async_copy(stage.at[slot], stage.at[slot], sem.at[slot]).wait()
    out_ref[...] = stage[slot].astype(BF16)


def unpack(me, whole, halved):
    pieces = len(whole) + len(halved)
    rows, n = whole[0].shape
    flat = list(whole) + [v for pair in halved for v in pair]
    return pl.pallas_call(
        functools.partial(unpack_kernel, pieces, len(halved)),
        grid_spec=pltpu.PrefetchScalarGridSpec(
            num_scalar_prefetch=1,
            grid=(pieces,),
            in_specs=[pl.BlockSpec(memory_space=pl.ANY)] * len(flat),
            out_specs=pl.BlockSpec((rows, n), lambda i, me: (i, 0)),
            scratch_shapes=[pltpu.VMEM((2, rows, n), F32), pltpu.SemaphoreType.DMA((2,))],
        ),
        out_shape=jax.ShapeDtypeStruct((rows * pieces, n), BF16),
        compiler_params=pltpu.CompilerParams(vmem_limit_bytes=VMEM),
        cost_estimate=cost(1, 6 * rows * pieces * n, 0),
        name="unpack",
    )(me, *flat)


def heads_fwd_kernel(heads, hdim, x_ref, lng_ref, wa_ref, qg_ref, kg_ref, qt_ref, kt_ref, vt_ref, wt_ref):
    inner = heads * hdim

    @pl.when(pl.program_id(0) == 0)
    def _():
        wt_ref[...] = wa_ref[:, : 3 * inner].T

    qkv = mm(wt_ref[...], layer_norm(x_ref, lng_ref), NT)
    qt_ref[...] = head_norm(qkv[:inner], qg_ref[...], heads, hdim)[0]
    kt_ref[...] = head_norm(qkv[inner : 2 * inner], kg_ref[...], heads, hdim)[0]
    vt_ref[...] = qkv[2 * inner :].astype(BF16)


def heads_fwd(x, lng, wa, qg, kg, heads, hdim, tm=512):
    tokens, width = x.shape
    inner = heads * hdim
    row = pl.BlockSpec((tm, width), lambda i: (i, 0))
    col = pl.BlockSpec((inner, tm), lambda i: (0, i))
    whole = lambda a: pl.BlockSpec(a.shape, lambda i: (0,) * a.ndim, pipeline_mode=pl.Buffered(1))
    return pl.pallas_call(
        functools.partial(heads_fwd_kernel, heads, hdim),
        grid=(tokens // tm,),
        in_specs=[row, whole(lng), whole(wa), whole(qg), whole(kg)],
        out_specs=[col, col, col],
        out_shape=[jax.ShapeDtypeStruct((inner, tokens), BF16)] * 3,
        scratch_shapes=[pltpu.VMEM((3 * inner, width), BF16)],
        compiler_params=pltpu.CompilerParams(vmem_limit_bytes=VMEM),
        cost_estimate=cost(6 * tokens * width * inner, tokens * (width * 2 + inner * 6), 0),
        name="heads_fwd",
    )(x, lng, wa, qg, kg)


def attend_fwd_kernel(hdim, bq, nh, qt_ref, kt_ref, vt_ref, vrow_ref, o_ref, ot_s, kn_s, vs_s):
    tokens = qt_ref.shape[1]
    vrow = vrow_ref[0]
    vrow_b = vrow.astype(BF16)
    sub = lax.broadcasted_iota(jnp.int32, (16, tokens), 0)
    ones_row = jnp.where(sub == 0, jnp.broadcast_to(vrow, (16, tokens)), 0.0).astype(BF16)
    for h in range(nh):
        rows = slice(h * hdim, (h + 1) * hdim)
        kn_s[h] = kt_ref[rows, :].T
        vs_s[h, :hdim, :] = vt_ref[rows, :] * vrow_b
        vs_s[h, hdim:, :] = ones_row

    def block(i, _):
        at = pl.ds(pl.multiple_of(i * bq, bq), bq)
        es = [jnp.exp2(mm(kn_s[h], qt_ref[h * hdim : (h + 1) * hdim, at])).astype(BF16) for h in range(nh)]
        for h in range(nh):
            oa = mm(vs_s[h], es[h])
            ot_s[h * hdim : (h + 1) * hdim, at] = (oa[:hdim, :] * (1.0 / oa[hdim : hdim + 1, :])).astype(BF16)
        return 0

    lax.fori_loop(0, tokens // bq, block, 0, unroll=True)
    o_ref[...] = ot_s[...].T


def attend_fwd(qt, kt, vt, vrow, heads, hdim, image, slots, bq=256, nh=2):
    inner = heads * hdim
    w = nh * hdim
    tcol = pl.BlockSpec((w, slots), lambda p: (p, image))
    return pl.pallas_call(
        functools.partial(attend_fwd_kernel, hdim, bq, nh),
        grid=(heads // nh,),
        in_specs=[tcol, tcol, tcol, pl.BlockSpec((1, 1, slots), lambda p: (0, 0, 0))],
        out_specs=pl.BlockSpec((slots, w), lambda p: (0, p)),
        out_shape=jax.ShapeDtypeStruct((slots, inner), BF16),
        scratch_shapes=[pltpu.VMEM((w, slots), BF16), pltpu.VMEM((nh, slots, hdim), BF16), pltpu.VMEM((nh, hdim + 16, slots), BF16)],
        compiler_params=pltpu.CompilerParams(vmem_limit_bytes=VMEM),
        cost_estimate=cost(heads * 2 * 8 * slots * slots * hdim, 8 * slots * inner, heads * slots * slots),
        name="attend_fwd",
    )(qt, kt, vt, vrow)


def out_rows_kernel(inner, bounds, x_ref, dz_ref, lng_ref, w_ref, wa_ref, wb_ref, o_ref, hid_ref, of_ref, *refs):
    near, far = refs[: len(bounds)], refs[len(bounds) : 2 * len(bounds)]
    out_ref, din_ref = refs[-2:]
    x = x_ref[...].astype(F32)
    centre = x - jnp.mean(x, axis=-1, keepdims=True)
    r = lax.rsqrt(jnp.mean(centre * centre, axis=-1, keepdims=True) + EPS)
    n = centre * r
    scaled = n * lng_ref[...]
    xn = scaled.astype(BF16)
    hidden = wb_ref.shape[1] // 2
    total = mm(o_ref[...], w_ref[:inner, :]) + mm(hid_ref[...], w_ref[inner:, :]) + mm(of_ref[...], wa_ref[...], NT)
    parts = []
    for c in range(0, hidden, 512):
        parts.append(gelu_parts(mm(xn, wb_ref[:, c : c + 512]))[0].astype(BF16))
    total = total + mm(jnp.concatenate(parts, axis=1), wb_ref[:, hidden:], NT)
    out_ref[...] = (x + total).astype(BF16)
    g = near[-1][...] + far[-1][...]
    for k in range(len(bounds) - 2, -1, -1):
        g = jnp.where(pl.program_id(0) < bounds[k], near[k][...] + far[k][...], g)
    a = g * lng_ref[...]
    back = r * (a - jnp.mean(a, axis=-1, keepdims=True) - n * jnp.mean(a * n, axis=-1, keepdims=True))
    din_ref[...] = (dz_ref[...].astype(F32) + back).astype(BF16)


def out_rows(x, dz, lng, wout, wa, wb, o, hid, of, near, far, image, prior, tm=256):
    slots, inner = o.shape
    go, width = wout.shape
    steps = slots // tm
    row = lambda n: pl.BlockSpec((tm, n), lambda i: (i, 0))
    at = pl.BlockSpec((tm, width), lambda i: (image * steps + i, 0))
    whole = lambda a: pl.BlockSpec(a.shape, lambda i: (0,) * a.ndim, pipeline_mode=pl.Buffered(1))
    specs, bounds = [], []
    for h in near:
        low, count = (bounds[-1] if bounds else 0), h.shape[0] // tm
        specs.append(pl.BlockSpec((tm, width), lambda i, low=low, count=count: (jnp.clip(i - low, 0, count - 1), 0)))
        bounds.append(low + count)
    given = [x, dz, lng, wout, wa, wb, o, hid, of, *near, *far]
    return pl.pallas_call(
        functools.partial(out_rows_kernel, inner, tuple(bounds)),
        grid=(steps,),
        in_specs=[at, at, whole(lng), whole(wout), pl.BlockSpec((width, inner), lambda i: (0, 3), pipeline_mode=pl.Buffered(1)), whole(wb), row(inner), row(go - inner), row(inner)]
        + specs
        + specs
        + [pl.BlockSpec(memory_space=pl.ANY)] * len(prior),
        out_specs=[at, at],
        out_shape=[jax.ShapeDtypeStruct(x.shape, BF16)] * 2,
        input_output_aliases={len(given) + k: k for k in range(len(prior))},
        compiler_params=pltpu.CompilerParams(vmem_limit_bytes=VMEM),
        cost_estimate=cost(2 * slots * width * (go + inner + wb.shape[1]), slots * (4 * go + 4 * width), slots * go),
        name="out_rows",
    )(*given, *prior)


def early_kernel(seqs, half, *refs):
    dzt, xnt, hid, du, out = refs[:seqs], refs[seqs : 2 * seqs], refs[2 * seqs : 3 * seqs], refs[3 * seqs : 4 * seqs], refs[-1]

    def total(left, right):
        out[...] = sum(mm(left[s][...], right[s][...]) for s in range(seqs))

    @pl.when(pl.program_id(0) < half)
    def _():
        total(dzt, hid)

    @pl.when(pl.program_id(0) >= half)
    def _():
        total(xnt, du)


def early_grads(dzt, xnt, hid, du, tn=512):
    seqs = len(hid)
    width, slots = xnt[0].shape
    hidden = hid[0].shape[1]
    half = hidden // tn
    res = pl.BlockSpec((width, slots), lambda j: (0, 0), pipeline_mode=pl.Buffered(1))
    return pl.pallas_call(
        functools.partial(early_kernel, seqs, half),
        grid=(2 * half,),
        in_specs=[res] * (2 * seqs)
        + [pl.BlockSpec((slots, tn), lambda j: (0, jnp.minimum(j, half - 1)))] * seqs
        + [pl.BlockSpec((slots, tn), lambda j: (0, jnp.maximum(j - half, 0)))] * seqs,
        out_specs=pl.BlockSpec((width, tn), lambda j: (0, j)),
        out_shape=jax.ShapeDtypeStruct((width, 2 * hidden), F32),
        compiler_params=pltpu.CompilerParams(vmem_limit_bytes=VMEM),
        cost_estimate=cost(flops=4 * seqs * slots * width * hidden, bytes_accessed=4 * seqs * slots * (width + hidden) + 8 * width * hidden, transcendentals=0),
        name="early_grads",
    )(*dzt, *xnt, *hid, *du)


def late_kernel(seqs, *refs):
    dzt, xnt = refs[:seqs], refs[seqs : 2 * seqs]
    o, dq, dk, dv = (refs[(2 + k) * seqs : (3 + k) * seqs] for k in range(4))
    small, out = refs[-2:]
    width = o[0].shape[1]
    for k, (left, right) in enumerate(((dzt, o), (xnt, dq), (xnt, dk), (xnt, dv))):
        out[:, k * width : (k + 1) * width] = sum(mm(left[s][...], right[s][...]) for s in range(seqs))
    out[:, 4 * width :] = small[...]


def late_grads(dzt, xnt, o, dq, dk, dv, small, tm=256):
    seqs = len(o)
    width, slots = xnt[0].shape
    inner = o[0].shape[1]
    left = pl.BlockSpec((tm, slots), lambda i: (i, 0))
    whole = pl.BlockSpec((slots, inner), lambda i: (0, 0), pipeline_mode=pl.Buffered(1))
    wide = 4 * inner + small.shape[1]
    return pl.pallas_call(
        functools.partial(late_kernel, seqs),
        grid=(width // tm,),
        in_specs=[left] * (2 * seqs) + [whole] * (4 * seqs) + [pl.BlockSpec((tm, small.shape[1]), lambda i: (i, 0))],
        out_specs=pl.BlockSpec((tm, wide), lambda i: (i, 0)),
        out_shape=jax.ShapeDtypeStruct((width, wide), F32),
        compiler_params=pltpu.CompilerParams(vmem_limit_bytes=VMEM),
        cost_estimate=cost(flops=8 * seqs * slots * width * inner, bytes_accessed=4 * seqs * slots * (width + 2 * inner) + 4 * width * wide, transcendentals=0),
        name="late_grads",
    )(*dzt, *xnt, *o, *dq, *dk, *dv, small)


def gate(value, *done):
    return lax.optimization_barrier((value, *done))[0]


def small_terms(g_q, g_k, width, shards):
    heads, hdim = g_q.shape
    part = lambda v: v.reshape(heads, shards, hdim // shards).transpose(1, 0, 2).reshape(shards, -1)
    gains = jnp.concatenate([part(g_q), part(g_k)], axis=1)
    gains = jnp.pad(gains, ((0, 0), (0, width // shards - gains.shape[1]))).reshape(width, 1)
    return jnp.pad(gains, ((0, 0), (0, 127)))


def per_device(shards, patches, keep_mask, counts, ln_gain, w_in, q_gain, k_gain, w_out, d_out):
    seqs, slots, width = patches.shape
    heads, hdim = q_gain.shape
    inner = heads * hdim
    swap = [(0, 1), (1, 0)]
    scale = hdim ** (-0.5)
    win, wout = w_in[0], w_out[0]
    hidden = wout.shape[0] - inner
    x = patches.reshape(seqs * slots, width)
    dz = d_out.reshape(seqs * slots, width)
    slot_ids = jnp.arange(slots, dtype=jnp.int32)
    valid = (slot_ids[None, :] < counts[:, None]) & ((keep_mask == 1) | (slot_ids[None, :] == 0))
    vrow = valid.astype(F32).reshape(seqs, 1, 1, slots)
    qg = q_gain.reshape(inner, 1)
    kg = k_gain.reshape(inner, 1)
    lng = ln_gain.reshape(1, width)
    qgs = qg * (scale * LOG2E)
    across = lambda v: lax.ppermute(v, "head", swap)

    def pair(v, bit):
        return lax.ppermute(v, "dp", [(i, i ^ bit) for i in range(shards)])

    def spread(v):
        return [pair(v, bit) for bit in (2, 4, 6)]

    bits = (2, 4, 1)
    me = lax.axis_index("dp")
    mine = sum(((me // bit) % 2) * 2**k for k, bit in enumerate(bits)).astype(jnp.int32)
    blk = width // 2 ** len(bits)
    rows = lax.dynamic_slice(win, (mine * blk, 0), (blk, win.shape[1])).astype(F32)
    cols = lax.dynamic_slice(wout, (0, mine * blk), (wout.shape[0], blk)).astype(F32).T
    piece_a = jnp.concatenate([rows[:, : 3 * inner], cols[:, :inner]], axis=1)
    piece_b = jnp.concatenate([rows[:, 3 * inner :], cols[:, inner:]], axis=1)
    gains = across(jnp.concatenate([qgs, kg], axis=0).reshape(-1, 128))
    a = [across(piece_a)]
    b = [across(gate(piece_b, a[0]))]

    def run(s, x):
        return project(x, dz, lng, win, wout, qgs, kg, heads, hdim, s, slots)

    order = [1, 2] + [2**k for k in range(shards.bit_length() - 2, 1, -1)]

    def halves(v, stage):
        left = sorted(order[stage:], reverse=True)
        v = v.reshape((2,) * len(left) + (width // shards, -1))
        axis = left.index(order[stage])
        bit = (me // order[stage]) % 2
        return lax.dynamic_index_in_dim(v, bit, axis, False), lax.dynamic_index_in_dim(v, 1 - bit, axis, False)

    def heads_of(s, p, first):
        xnt, dzt, qt, kt, vt, dot, rq, rk, hid, du = p
        return attend(first, kt, vt, dot, rq, rk, vrow[s], qg, kg, heads, hdim, slots)

    p0 = run(0, x)
    o0, dq0, dk0, dv0, gq0, gk0 = heads_of(0, p0, gate(p0[2], *a))
    a += spread(a[0])
    quarter = slots // 4
    cuts = (0, quarter, 2 * quarter, slots)
    n0 = back_rows(gate(dq0, *a, *b, gains), dk0, dv0, p0[9], win, cuts)
    a += [pair(gate(v, dq0), 1) for v in a]
    b += spread(b[0])
    n0 = list(n0)
    n0[0] = gate(n0[0], *a)
    f0 = [across(v) for v in n0]
    p1 = run(1, gate(x, n0[0]))
    early = early_grads(*[[gate(p[k], f0[0]) if p is p1 else p[k] for p in (p0, p1)] for k in (1, 0, 8, 9)])
    early = gate(early, f0[1], *b[:3])
    early_rs = lax.psum_scatter(early, "dp", scatter_dimension=0, tiled=True)
    o1, dq1, dk1, dv1, gq1, gk1 = heads_of(1, p1, gate(p1[2], early))
    n1 = back_rows(gate(dq1, b[3]), dk1, dv1, p1[9], win, cuts)
    n1 = list(n1)
    n1[0] = gate(n1[0], f0[2])
    b += [pair(gate(v, dq1), 1) for v in b]
    small = small_terms((gq0 + gq1).reshape(heads, hdim), (gk0 + gk1).reshape(heads, hdim), width, shards)
    late = late_grads([p0[1], p1[1]], [p0[0], p1[0]], [o0, o1], [gate(dq0, n1[0]), dq1], [dk0, dk1], [dv0, dv1], small)
    f1 = [across(v) for v in n1]
    late = gate(late, f1[0])
    mine = mine.reshape(1)
    wa = unpack(mine, [gate(a[0], late)] + a[1:], [])
    keep, send = halves(late, 0)
    got = pair(send, order[0])
    gains = gains.reshape(-1, 1)
    qf, kf, vf = heads_fwd(gate(x, wa, got), lng, wa, gains[:inner], gains[inner:], heads, hdim)
    keep, send = halves(keep + got, 1)
    got = pair(send, order[1])
    of0 = attend_fwd(gate(qf, f1[1]), kf, vf, vrow[0], heads, hdim, 0, slots)
    of1 = attend_fwd(gate(qf, of0), kf, vf, vrow[1], heads, hdim, 1, slots)
    wb = unpack(mine, [gate(b[0], of1, got)] + b[1:], [])
    keep, send = halves(keep + gate(got, of1), 2)
    got = pair(send, order[2])
    outs = out_rows(gate(x, wb), dz, lng, wout, wa, wb, o0, p0[8], of0, n0, f0, 0, [])
    got = gate(got, outs[0])
    for stage in range(3, len(order)):
        keep, send = halves(keep + got, stage)
        got = pair(send, order[stage])
    bo, d_in = out_rows(gate(x, outs[0], f1[2]), dz, lng, wout, wa, wb, o1, p1[8], of1, n1, f1, 1, outs)
    late_rs = (keep + got).reshape(width // shards, -1)
    block_output = bo.reshape(patches.shape)
    d_in = d_in.reshape(patches.shape)
    g_w_out = jnp.concatenate([late_rs[:, :inner], early_rs[:, :hidden]], axis=1).T[None]
    g_w_in = jnp.concatenate([late_rs[:, inner : 4 * inner], early_rs[:, hidden:]], axis=1)[None]
    band = lambda v: lax.dynamic_slice_in_dim(v, me * (width // shards), width // shards, 0)
    g_ln = jnp.sum(band(win).astype(F32) * g_w_in[0], axis=1) / band(ln_gain)
    g_ln = g_ln + across(g_ln)
    terms = late_rs[:, 4 * inner]
    count = inner // shards
    g_q = terms[:count].reshape(heads, hdim // shards)
    g_k = terms[count : 2 * count].reshape(heads, hdim // shards)
    return block_output, d_in, g_ln, g_w_in, g_q, g_k, g_w_out


def solution(mesh):
    placed = (
        P("dp", None, None),
        P("dp", None),
        P("dp"),
        P(),
        P("head", None, None),
        P("head", None),
        P("head", None),
        P("head", None, None),
        P("dp", None, None),
    )
    return jax.shard_map(
        functools.partial(per_device, mesh.shape["dp"]),
        mesh=mesh,
        in_specs=placed,
        out_specs=(
            P("dp", None, None),
            P("dp", None, None),
            P("dp"),
            P("head", "dp", None),
            P("head", "dp"),
            P("head", "dp"),
            P("head", None, "dp"),
        ),
        check_vma=False,
    )
```

```python
import functools
import math

import jax
import jax.numpy as jnp
from jax import lax
from jax.experimental import pallas as pl
from jax.experimental.pallas import tpu as pltpu
from jax.sharding import PartitionSpec as P

EPS = 1e-06
LOG2E = 1.4426950408889634
F32 = jnp.float32
BF16 = jnp.bfloat16
VMEM = 67000000
COST = 560
BQ = 512
UNROLL = 1
NT = (((1,), (1,)), ((), ()))
NN = (((1,), (0,)), ((), ()))


def cost(us):
    return pl.CostEstimate(flops=int(us * COST * 1e6), bytes_accessed=1, transcendentals=0)


def mm(a, b, dims=NN):
    return lax.dot_general(a, b, dims, preferred_element_type=F32)


def gelu_parts(u):
    cdf = 0.5 + 0.5 * lax.erf(u * math.sqrt(0.5))
    return u * cdf, cdf + u * (jnp.exp2(u * u * (-0.5 * LOG2E)) * (1.0 / math.sqrt(2.0 * math.pi)))


def head_norm(v, gain, heads, hdim):
    tokens = v.shape[-1]
    v = v.reshape(heads, hdim, tokens)
    centre = v - jnp.mean(v, axis=1, keepdims=True)
    r = lax.rsqrt(jnp.mean(centre * centre, axis=1, keepdims=True) + EPS)
    n = (centre * r).reshape(heads * hdim, tokens)
    return (n * gain).astype(BF16), r


def layer_norm(x_ref, lng_ref):
    x = x_ref[...].astype(F32)
    centre = x - jnp.mean(x, axis=-1, keepdims=True)
    r = lax.rsqrt(jnp.mean(centre * centre, axis=-1, keepdims=True) + EPS)
    return (centre * r * lng_ref[...]).astype(BF16)


def project_kernel(heads, hdim, first_ref, x_ref, dz_ref, lng_ref, win_ref, wout_ref, qg_ref, kg_ref,
                   left_ref, qt_ref, kt_ref, vt_ref, dot_ref, rq_ref, rk_ref, right_ref, wt_ref, xn_ref):
    inner = heads * hdim
    now = lax.rem(pl.program_id(0), 2)

    @pl.when(pl.program_id(0) == 0)
    def _():
        wt_ref[...] = win_ref[:, : 3 * inner].T
        xn_ref[0] = layer_norm(first_ref, lng_ref)

    xn = xn_ref[now]
    xn_ref[1 - now] = layer_norm(x_ref, lng_ref)
    dz = dz_ref[...]
    width = dz.shape[1]
    left_ref[:width, :] = dz.T
    left_ref[width:, :] = xn.T
    qkv = mm(wt_ref[...], xn, NT)
    qn, rq = head_norm(qkv[:inner], qg_ref[...], heads, hdim)
    kn, rk = head_norm(qkv[inner : 2 * inner], kg_ref[...], heads, hdim)
    qt_ref[...] = qn
    kt_ref[...] = kn
    rq_ref[...] = rq
    rk_ref[...] = rk
    vt_ref[...] = qkv[2 * inner :].astype(BF16)
    dot_ref[...] = mm(wout_ref[:inner, :], dz, NT).astype(BF16)
    hidden = win_ref.shape[1] - 3 * inner
    step = 512
    for c in range(0, hidden, step):
        u = mm(xn, win_ref[:, 3 * inner + c : 3 * inner + c + step])
        dh = mm(dz, wout_ref[inner + c : inner + c + step, :], NT)
        h, slope = gelu_parts(u)
        right_ref[:, c : c + step] = h.astype(BF16)
        right_ref[:, hidden + c : hidden + c + step] = (dh * slope).astype(BF16)


def project(x, dz, lng, win, wout, qg, kg, heads, hdim, tm=256):
    tokens, width = x.shape
    inner = heads * hdim
    gw = win.shape[1]
    hidden = gw - 3 * inner
    steps = tokens // tm
    given = lambda f: pl.BlockSpec((tm, width), lambda i: (f(i), 0))
    col = lambda n: pl.BlockSpec((n, tm), lambda i: (0, i))
    whole = lambda a: pl.BlockSpec(a.shape, lambda i: (0,) * a.ndim, pipeline_mode=pl.Buffered(1))
    stat = pl.BlockSpec((heads, 1, tm), lambda i: (0, 0, i))
    sds = jax.ShapeDtypeStruct
    return pl.pallas_call(
        functools.partial(project_kernel, heads, hdim),
        grid=(steps,),
        in_specs=[given(lambda i: 0), given(lambda i: jnp.minimum(i + 1, steps - 1)), given(lambda i: i), whole(lng), whole(win), whole(wout), whole(qg), whole(kg)],
        out_specs=[col(2 * width), col(inner), col(inner), col(inner), col(inner), stat, stat, pl.BlockSpec((tm, 2 * hidden), lambda i: (i, 0))],
        out_shape=[sds((2 * width, tokens), BF16)]
        + [sds((inner, tokens), BF16)] * 4
        + [sds((heads, 1, tokens), F32)] * 2
        + [sds((tokens, 2 * hidden), BF16)],
        scratch_shapes=[pltpu.VMEM((3 * inner, width), BF16), pltpu.VMEM((2, tm, width), BF16)],
        compiler_params=pltpu.CompilerParams(vmem_limit_bytes=VMEM),
        cost_estimate=cost(28),
        name="project",
    )(x, x, dz, lng, win, wout, qg, kg)


def attend_kernel(hdim, bq, nh, image_ref, qt_ref, kt_ref, vt_ref, dot_ref, rq_ref, rk_ref, vrow_ref, qg_ref, kg_ref,
                  o_ref, dq_ref, dk_ref, dv_ref, gq_ref, gk_ref, dqt_s, dkt_s, dvt_s, ot_s, kn_s, ktv_s, vs_s, va_s):
    tokens = qt_ref.shape[1]
    vrow = vrow_ref[0]
    vrow_b = vrow.astype(BF16)
    scale = hdim ** (-0.5)
    sub = lax.broadcasted_iota(jnp.int32, (16, tokens), 0)
    ones_row = jnp.where(sub == 0, jnp.broadcast_to(vrow, (16, tokens)), 0.0).astype(BF16)
    minus_row = jnp.where(sub < 2, 1.0, 0.0).astype(BF16)
    ktv_s[...] = kt_ref[...] * vrow_b
    for h in range(nh):
        rows = slice(h * hdim, (h + 1) * hdim)
        vt = vt_ref[rows, :]
        kn_s[h] = kt_ref[rows, :].T
        vs_s[h, :hdim, :] = vt * vrow_b
        vs_s[h, hdim:, :] = ones_row
        va_s[h] = jnp.concatenate([vt, minus_row], axis=0).T
    dkt_s[...] = jnp.zeros_like(dkt_s)
    dvt_s[...] = jnp.zeros_like(dvt_s)
    sub16 = lax.broadcasted_iota(jnp.int32, (16, bq), 0)

    def first(h, i):
        rows = slice(h * hdim, (h + 1) * hdim)
        at = pl.ds(pl.multiple_of(i * bq, bq), bq)
        return jnp.exp2(mm(kn_s[h], qt_ref[rows, at])).astype(BF16)

    def second(h, i, e):
        rows = slice(h * hdim, (h + 1) * hdim)
        at = pl.ds(pl.multiple_of(i * bq, bq), bq)
        qb = qt_ref[rows, at]
        dob = dot_ref[rows, at]
        oa = mm(vs_s[h], e)
        linv = 1.0 / oa[hdim : hdim + 1, :]
        o = oa[:hdim, :] * linv
        ot_s[rows, at] = o.astype(BF16)
        dof = dob.astype(F32)
        delta = jnp.sum(dof * o, axis=0, keepdims=True) * linv
        hi = delta.astype(BF16)
        lo = (delta - hi.astype(F32)).astype(BF16)
        dos = (dof * linv).astype(BF16)
        minus = jnp.where(sub16 == 0, -hi.astype(F32), jnp.where(sub16 == 1, -lo.astype(F32), 0.0)).astype(BF16)
        t = mm(va_s[h], jnp.concatenate([dos, minus], axis=0))
        ds = (e.astype(F32) * t).astype(BF16)
        dvt_s[rows, :] += mm(dos, e, NT)
        dkt_s[rows, :] += mm(qb, ds, NT)
        dqt_s[rows, at] = mm(ktv_s[rows, :], ds)

    def block(i, _):
        es = [first(h, i) for h in range(nh)]
        for h in range(nh):
            second(h, i, es[h])
        return 0

    lax.fori_loop(0, tokens // bq, block, 0, unroll=UNROLL)

    for p in range(nh // 2):
        prow = slice(p * 2 * hdim, (p + 1) * 2 * hdim)
        o_ref[:, prow] = ot_s[prow, :].T
        dv_ref[:, prow] = (dvt_s[prow, :] * vrow).astype(BF16).T
        for src, raw, r_ref, g_ref, grad_ref, dst, mul, c in (
            (dqt_s, qt_ref, rq_ref, qg_ref, gq_ref, dq_ref, scale, scale * LOG2E),
            (dkt_s, kt_ref, rk_ref, kg_ref, gk_ref, dk_ref, 1.0 / LOG2E, 1.0),
        ):
            both = []
            for h in (2 * p, 2 * p + 1):
                rows = slice(h * hdim, (h + 1) * hdim)
                g = g_ref[rows, :]
                inv = 1.0 / (g * c)
                d = src[rows, :]
                if raw is kt_ref:
                    d = d * vrow
                x = raw[rows, :].astype(F32)
                prod = d * x
                grad_ref[rows, :] = jnp.sum(prod, axis=1, keepdims=True) * (inv * mul)
                a = d * (g * mul)
                m1 = jnp.mean(a, axis=0, keepdims=True)
                m2 = jnp.mean(prod, axis=0, keepdims=True) * (mul / c)
                both.append((r_ref[h] * (a - m1 - (x * inv) * m2)).astype(BF16))
            dst[:, prow] = jnp.concatenate(both, axis=0).T

def attend(image, qt, kt, vt, dot, rq, rk, vrow, qg, kg, heads, hdim, slots, bq=BQ, nh=2):
    inner = heads * hdim
    w = nh * hdim
    sds = jax.ShapeDtypeStruct
    tcol = pl.BlockSpec((w, slots), lambda p, im: (p, im[0]))
    stat = pl.BlockSpec((nh, 1, slots), lambda p, im: (p, 0, im[0]))
    gain = pl.BlockSpec((w, 1), lambda p, im: (p, 0))
    row = pl.BlockSpec((slots, w), lambda p, im: (0, p))
    return pl.pallas_call(
        functools.partial(attend_kernel, hdim, min(bq, slots), nh),
        grid_spec=pltpu.PrefetchScalarGridSpec(
            num_scalar_prefetch=1,
            grid=(heads // nh,),
            in_specs=[tcol, tcol, tcol, tcol, stat, stat, pl.BlockSpec((1, 1, slots), lambda p, im: (im[0], 0, 0)), gain, gain],
            out_specs=[row, row, row, row, gain, gain],
            scratch_shapes=[pltpu.VMEM((w, slots), F32)] * 3
            + [
                pltpu.VMEM((w, slots), BF16),
                pltpu.VMEM((nh, slots, hdim), BF16),
                pltpu.VMEM((w, slots), BF16),
                pltpu.VMEM((nh, hdim + 16, slots), BF16),
                pltpu.VMEM((nh, slots, hdim + 16), BF16),
            ],
        ),
        out_shape=[sds((slots, inner), BF16)] * 4 + [sds((inner, 1), F32)] * 2,
        compiler_params=pltpu.CompilerParams(vmem_limit_bytes=VMEM),
        cost_estimate=cost(25),
        name="attend",
    )(image, qt, kt, vt, dot, rq, rk, vrow, qg, kg)


def overlaps(cuts, step, tm):
    for k in range(len(cuts) - 1):
        low, high = max(step * tm, cuts[k]), min((step + 1) * tm, cuts[k + 1])
        if low < high:
            yield k, low - cuts[k], low - step * tm, high - low


def back_rows_kernel(inner, cuts, steps, image_ref, dq_ref, dk_ref, dv_ref, du_ref, w_ref, *outs):
    g = (
        mm(dq_ref[...], w_ref[:, :inner], NT)
        + mm(dk_ref[...], w_ref[:, inner : 2 * inner], NT)
        + mm(dv_ref[...], w_ref[:, 2 * inner : 3 * inner], NT)
        + mm(du_ref[...], w_ref[:, 3 * inner :], NT)
    )
    if len(outs) == 1:
        outs[0][...] = g
        return
    for step in range(steps):

        @pl.when(pl.program_id(0) == step)
        def _(step=step):
            for k, at, low, n in overlaps(cuts, step, g.shape[0]):
                outs[k][at : at + n, :] = g[low : low + n]


def back_rows(image, dq, dk, dv, right, win, cuts, tm=256):
    slots, inner = dq.shape
    width, gw = win.shape
    hidden = gw - 3 * inner
    steps = slots // tm
    row = lambda n: pl.BlockSpec((tm, n), lambda i, im: (i, 0))
    parts = [b - a for a, b in zip(cuts, cuts[1:])]
    return pl.pallas_call(
        functools.partial(back_rows_kernel, inner, cuts, steps),
        grid_spec=pltpu.PrefetchScalarGridSpec(
            num_scalar_prefetch=1,
            grid=(steps,),
            in_specs=[row(inner)] * 3 + [pl.BlockSpec((tm, hidden), lambda i, im: (im[0] * steps + i, 1)), pl.BlockSpec(win.shape, lambda i, im: (0, 0), pipeline_mode=pl.Buffered(1))],
            out_specs=[pl.BlockSpec((n, width), lambda i, im: (0, 0)) for n in parts] if len(parts) > 1 else [row(width)],
        ),
        out_shape=[jax.ShapeDtypeStruct((n, width), F32) for n in parts],
        compiler_params=pltpu.CompilerParams(vmem_limit_bytes=VMEM),
        cost_estimate=cost(10),
        name="back_rows",
    )(image, dq, dk, dv, right, win)


def fetch(me, parts, stage, sem):
    rows = stage.shape[0] // len(parts)
    for k, refs in enumerate(parts):
        block = jnp.bitwise_xor(me, k)
        low = 0
        for ref in refs:
            pltpu.make_async_copy(ref, stage.at[pl.ds(pl.multiple_of(block * rows + low, 8), ref.shape[0])], sem.at[block]).start()
            low += ref.shape[0]


def grouped(counts, refs):
    out = []
    for n in counts:
        out.append(refs[:n])
        refs = refs[n:]
    return out


def arrived(block, rows, stage, sem):
    view = stage.at[pl.ds(pl.multiple_of(block * rows, 8), rows)]
    pltpu.make_async_copy(view, view, sem.at[block]).wait()


def unpack_kernel(counts, me_ref, *refs):
    parts, (out_ref, stage, sem) = grouped(counts, refs[:-3]), refs[-3:]
    step = pl.program_id(0)
    rows = out_ref.shape[0]

    @pl.when(step == 0)
    def _():
        fetch(me_ref[0], parts, stage, sem)

    arrived(step, rows, stage, sem)
    out_ref[...] = stage[pl.ds(pl.multiple_of(step * rows, 8), rows), :].astype(BF16)


def unpack(me, parts):
    pieces = len(parts)
    flat = [v for part in parts for v in part]
    rows, n = sum(v.shape[0] for v in parts[0]), flat[0].shape[1]
    return pl.pallas_call(
        functools.partial(unpack_kernel, tuple(len(part) for part in parts)),
        grid_spec=pltpu.PrefetchScalarGridSpec(
            num_scalar_prefetch=1,
            grid=(pieces,),
            in_specs=[pl.BlockSpec(memory_space=pl.ANY)] * len(flat),
            out_specs=pl.BlockSpec((rows, n), lambda i, me: (i, 0)),
            scratch_shapes=[pltpu.VMEM((rows * pieces, n), F32), pltpu.SemaphoreType.DMA((pieces,))],
        ),
        out_shape=jax.ShapeDtypeStruct((rows * pieces, n), BF16),
        compiler_params=pltpu.CompilerParams(vmem_limit_bytes=VMEM),
        cost_estimate=cost(6),
        name="unpack",
    )(me, *flat)


def heads_fwd_kernel(heads, hdim, me_ref, qg_ref, kg_ref, xnt_ref, *refs):
    parts, (qt_ref, kt_ref, vt_ref, wo_ref, _, _, wt_ref, stage, sem) = refs[:-9], refs[-9:]
    inner = heads * hdim

    @pl.when(pl.program_id(0) == 0)
    def _():
        fetch(me_ref[0], [(ref,) for ref in parts], stage, sem)
        for k in range(len(parts)):
            arrived(k, parts[0].shape[0], stage, sem)
        wt_ref[...] = stage[:, : 3 * inner].astype(BF16).T
        wo_ref[...] = stage[:, 3 * inner :].astype(BF16)

    qkv = mm(wt_ref[...], xnt_ref[...])
    qt_ref[...] = head_norm(qkv[:inner], qg_ref[...], heads, hdim)[0]
    kt_ref[...] = head_norm(qkv[inner : 2 * inner], kg_ref[...], heads, hdim)[0]
    vt_ref[...] = qkv[2 * inner :].astype(BF16)


def heads_fwd(me, qg, kg, left, parts, heads, hdim, tm=512):
    width, tokens = left.shape[0] // 2, left.shape[1]
    inner = heads * hdim
    n = parts[0].shape[1]
    col = pl.BlockSpec((inner, tm), lambda i, me: (0, i))
    gain = pl.BlockSpec((inner, 1), lambda i, me: (0, 0))
    out = pl.BlockSpec((width, inner), lambda i, me: (0, 0))
    raw = pl.BlockSpec(memory_space=pl.ANY)
    sds = jax.ShapeDtypeStruct
    return pl.pallas_call(
        functools.partial(heads_fwd_kernel, heads, hdim),
        grid_spec=pltpu.PrefetchScalarGridSpec(
            num_scalar_prefetch=1,
            grid=(tokens // tm,),
            in_specs=[gain, gain, pl.BlockSpec((width, tm), lambda i, me: (1, i))] + [raw] * len(parts),
            out_specs=[col, col, col, out, raw, raw],
            scratch_shapes=[pltpu.VMEM((3 * inner, width), BF16), pltpu.VMEM((width, n), F32), pltpu.SemaphoreType.DMA((len(parts),))],
        ),
        out_shape=[sds((inner, tokens), BF16)] * 3 + [sds((width, inner), BF16)] + [sds((tokens, width), BF16)] * 2,
        compiler_params=pltpu.CompilerParams(vmem_limit_bytes=VMEM),
        cost_estimate=cost(10),
        name="heads_fwd",
    )(me, qg, kg, left, *parts)


def attend_fwd_kernel(hdim, bq, nh, qt_ref, kt_ref, vt_ref, vrow_ref, o_ref, ot_s, kn_s, vs_s):
    tokens = qt_ref.shape[1]
    vrow = vrow_ref[0]
    vrow_b = vrow.astype(BF16)
    sub = lax.broadcasted_iota(jnp.int32, (16, tokens), 0)
    ones_row = jnp.where(sub == 0, jnp.broadcast_to(vrow, (16, tokens)), 0.0).astype(BF16)
    for h in range(nh):
        rows = slice(h * hdim, (h + 1) * hdim)
        kn_s[h] = kt_ref[rows, :].T
        vs_s[h, :hdim, :] = vt_ref[rows, :] * vrow_b
        vs_s[h, hdim:, :] = ones_row

    def block(i, _):
        at = pl.ds(pl.multiple_of(i * bq, bq), bq)
        es = [jnp.exp2(mm(kn_s[h], qt_ref[h * hdim : (h + 1) * hdim, at])).astype(BF16) for h in range(nh)]
        for h in range(nh):
            oa = mm(vs_s[h], es[h])
            ot_s[h * hdim : (h + 1) * hdim, at] = (oa[:hdim, :] * (1.0 / oa[hdim : hdim + 1, :])).astype(BF16)
        return 0

    lax.fori_loop(0, tokens // bq, block, 0, unroll=True)
    o_ref[...] = ot_s[...].T


def attend_fwd(qt, kt, vt, vrow, heads, hdim, slots, bq=BQ, nh=2):
    inner = heads * hdim
    w = nh * hdim
    seqs = qt.shape[1] // slots
    tcol = pl.BlockSpec((w, slots), lambda s, p: (p, s))
    return pl.pallas_call(
        functools.partial(attend_fwd_kernel, hdim, min(bq, slots), nh),
        grid=(seqs, heads // nh),
        in_specs=[tcol, tcol, tcol, pl.BlockSpec((1, 1, slots), lambda s, p: (s, 0, 0))],
        out_specs=pl.BlockSpec((slots, w), lambda s, p: (s, p)),
        out_shape=jax.ShapeDtypeStruct((seqs * slots, inner), BF16),
        scratch_shapes=[pltpu.VMEM((w, slots), BF16), pltpu.VMEM((nh, slots, hdim), BF16), pltpu.VMEM((nh, hdim + 16, slots), BF16)],
        compiler_params=pltpu.CompilerParams(vmem_limit_bytes=VMEM),
        cost_estimate=cost(16),
        name="attend_fwd",
    )(qt, kt, vt, vrow)


def out_rows_kernel(inner, cuts, steps, image_ref, x_ref, dz_ref, lng_ref, w_ref, wa_ref, wb_ref, o_ref, hid_ref, of_ref, *refs):
    pieces = len(cuts) - 1
    near, far = refs[:pieces], refs[pieces : 2 * pieces]
    out_ref, din_ref, both, sem = refs[-4:]
    tm = x_ref.shape[0]
    now = pl.program_id(0)

    @pl.when(now == 0)
    def _():
        for step in range(steps):
            for k, at, low, n in overlaps(cuts, step, tm):
                for side, parts in enumerate((near, far)):
                    pltpu.make_async_copy(parts[k].at[pl.ds(at, n)], both.at[step, side, pl.ds(low, n)], sem.at[step]).start()

    x = x_ref[...].astype(F32)
    centre = x - jnp.mean(x, axis=-1, keepdims=True)
    r = lax.rsqrt(jnp.mean(centre * centre, axis=-1, keepdims=True) + EPS)
    n = centre * r
    scaled = n * lng_ref[...]
    xn = scaled.astype(BF16)
    hidden = wb_ref.shape[1] // 2
    total = mm(o_ref[...], w_ref[:inner, :]) + mm(hid_ref[...], w_ref[inner:, :]) + mm(of_ref[...], wa_ref[...], NT)
    parts = []
    for c in range(0, hidden, 512):
        parts.append(gelu_parts(mm(xn, wb_ref[:, c : c + 512]))[0].astype(BF16))
    total = total + mm(jnp.concatenate(parts, axis=1), wb_ref[:, hidden:], NT)
    out_ref[...] = (x + total).astype(BF16)
    pltpu.make_async_copy(both.at[now], both.at[now], sem.at[now]).wait()
    a = (both[now, 0] + both[now, 1]) * lng_ref[...]
    back = r * (a - jnp.mean(a, axis=-1, keepdims=True) - n * jnp.mean(a * n, axis=-1, keepdims=True))
    din_ref[...] = (dz_ref[...].astype(F32) + back).astype(BF16)


def out_rows(image, x, dz, lng, wout, wa, wb, o, right, of, near, far, cuts, prior, tm=256):
    slots, inner = o.shape
    go, width = wout.shape
    steps = slots // tm
    row = lambda n: pl.BlockSpec((tm, n), lambda i, im: (i, 0))
    of_image = lambda n: pl.BlockSpec((tm, n), lambda i, im: (im[0] * steps + i, 0))
    at = of_image(width)
    whole = lambda a: pl.BlockSpec(a.shape, lambda i, im: (0,) * a.ndim, pipeline_mode=pl.Buffered(1))
    given = [image, x, dz, lng, wout, wa, wb, o, right, of, *near, *far]
    raw = pl.BlockSpec(memory_space=pl.ANY)
    return pl.pallas_call(
        functools.partial(out_rows_kernel, inner, cuts, steps),
        grid_spec=pltpu.PrefetchScalarGridSpec(
            num_scalar_prefetch=1,
            grid=(steps,),
            in_specs=[at, at, whole(lng), whole(wout), whole(wa), whole(wb), row(inner), of_image(go - inner), of_image(inner)] + [raw] * (len(near) + len(far) + 2),
            out_specs=[at, at],
            scratch_shapes=[pltpu.VMEM((steps, 2, tm, width), F32), pltpu.SemaphoreType.DMA((steps,))],
        ),
        out_shape=[jax.ShapeDtypeStruct(x.shape, BF16)] * 2,
        input_output_aliases={len(given) + k: k for k in range(2)},
        compiler_params=pltpu.CompilerParams(vmem_limit_bytes=VMEM),
        cost_estimate=cost(18),
        name="out_rows",
    )(*given, *prior)


def early_kernel(left_ref, right_ref, out_ref):
    out_ref[...] = mm(left_ref[...], right_ref[...])


def early_grads(left, right, tn=512):
    width, tokens = left.shape[0] // 2, left.shape[1]
    both = right.shape[1]
    steps = both // tn
    return pl.pallas_call(
        early_kernel,
        grid=(steps,),
        in_specs=[pl.BlockSpec((width, tokens), lambda j: (jnp.where(j < steps // 2, 0, 1), 0)), pl.BlockSpec((tokens, tn), lambda j: (0, j))],
        out_specs=pl.BlockSpec((width, tn), lambda j: (0, j)),
        out_shape=jax.ShapeDtypeStruct((width, both), F32),
        compiler_params=pltpu.CompilerParams(vmem_limit_bytes=VMEM),
        cost_estimate=cost(16),
        name="early_grads",
    )(left, right)


def late_kernel(seqs, low, core_ref, *refs):
    dzt, xnt = refs[:seqs], refs[seqs : 2 * seqs]
    o, dq, dk, dv = (refs[(2 + k) * seqs : (3 + k) * seqs] for k in range(4))
    small, keep, send = refs[-3:]
    width = o[0].shape[1]

    def store(cols, v):
        for half in range(2):
            rows = jnp.concatenate([v[b : b + low] for b in range(half * low, v.shape[0], 2 * low)], axis=0)

            @pl.when(core_ref[0] == half)
            def _():
                keep[:, cols] = rows

            @pl.when(core_ref[0] != half)
            def _():
                send[:, cols] = rows

    for k, (left, right) in enumerate(((dzt, o), (xnt, dq), (xnt, dk), (xnt, dv))):
        store(slice(k * width, (k + 1) * width), sum(mm(left[s][...], right[s][...]) for s in range(seqs)))
    store(slice(4 * width, 4 * width + small.shape[1]), small[...])


def late_grads(core, left, o, dq, dk, dv, small, low):
    seqs = len(o)
    slots, inner = o[0].shape
    width = left.shape[0] // 2
    tm = 4 * low
    while tm < 192:
        tm *= 2
    steps = width // tm
    above = [pl.BlockSpec((tm, slots), lambda i, c, s=s: (i, s)) for s in range(seqs)]
    below = [pl.BlockSpec((tm, slots), lambda i, c, s=s: (steps + i, s)) for s in range(seqs)]
    whole = pl.BlockSpec((slots, inner), lambda i, c: (0, 0), pipeline_mode=pl.Buffered(1))
    wide = 4 * inner + small.shape[1]
    out = pl.BlockSpec((tm // 2, wide), lambda i, c: (i, 0))
    return pl.pallas_call(
        functools.partial(late_kernel, seqs, low),
        grid_spec=pltpu.PrefetchScalarGridSpec(
            num_scalar_prefetch=1,
            grid=(steps,),
            in_specs=above + below + [whole] * (4 * seqs) + [pl.BlockSpec((tm, small.shape[1]), lambda i, c: (i, 0))],
            out_specs=[out, out],
        ),
        out_shape=[jax.ShapeDtypeStruct((width // 2, wide), F32)] * 2,
        compiler_params=pltpu.CompilerParams(vmem_limit_bytes=VMEM),
        cost_estimate=cost(12),
        name="late_grads",
    )(core, *[left] * (2 * seqs), *o, *dq, *dk, *dv, small)


def gate(value, *done):
    return lax.optimization_barrier((value, *done))[0]


def small_terms(g_q, g_k, width, shards):
    heads, hdim = g_q.shape
    part = lambda v: v.reshape(heads, shards, hdim // shards).transpose(1, 0, 2).reshape(shards, -1)
    gains = jnp.concatenate([part(g_q), part(g_k)], axis=1)
    gains = jnp.pad(gains, ((0, 0), (0, width // shards - gains.shape[1]))).reshape(width, 1)
    return jnp.pad(gains, ((0, 0), (0, 127)))


def per_device(shards, patches, keep_mask, counts, ln_gain, w_in, q_gain, k_gain, w_out, d_out):
    seqs, slots, width = patches.shape
    heads, hdim = q_gain.shape
    inner = heads * hdim
    swap = [(0, 1), (1, 0)]
    scale = hdim ** (-0.5)
    win, wout = w_in[0], w_out[0]
    hidden = wout.shape[0] - inner
    x = patches.reshape(seqs * slots, width)
    dz = d_out.reshape(seqs * slots, width)
    slot_ids = jnp.arange(slots, dtype=jnp.int32)
    valid = (slot_ids[None, :] < counts[:, None]) & ((keep_mask == 1) | (slot_ids[None, :] == 0))
    vrow = valid.astype(F32).reshape(seqs, 1, slots)
    qg = q_gain.reshape(inner, 1)
    kg = k_gain.reshape(inner, 1)
    lng = ln_gain.reshape(1, width)
    qgs = qg * (scale * LOG2E)
    across = lambda v: lax.ppermute(v, "head", swap)

    def pair(v, bit):
        return lax.ppermute(v, "dp", [(i, i ^ bit) for i in range(shards)])

    number = [jnp.full((1,), s, jnp.int32) for s in range(seqs)]
    me = lax.axis_index("dp")

    quarter = width // 4

    def rows_of(bit, left_cols, right_rows):
        mine = ((me // bit) % 2) + 2 * (me % 2)
        rows = lax.dynamic_slice(win, (mine * quarter, left_cols[0]), (quarter, left_cols[1] - left_cols[0]))
        cols = lax.dynamic_slice(wout, (right_rows[0], mine * quarter), (right_rows[1] - right_rows[0], quarter))
        return mine.astype(jnp.int32).reshape(1), jnp.concatenate([rows.astype(F32), cols.astype(F32).T], axis=1)

    mine_a, piece_a = rows_of(2, (0, 3 * inner), (0, inner))
    mine_b, piece_b = rows_of(4, (3 * inner, win.shape[1]), (inner, wout.shape[0]))
    gains = across(jnp.concatenate([qgs, kg], axis=0).reshape(-1, 128))
    a = [across(piece_a)]

    low = width // shards
    cell = lambda v, axis, at: lax.dynamic_index_in_dim(v, at, axis, False)
    others = shards // 4

    def by_two(v, w):
        bit = (me // 2) % 2
        v, w = (u.reshape(others, 2, low, -1) for u in (v, w))
        return cell(v, 1, bit) + cell(w, 1, bit), cell(v, 1, 1 - bit) + cell(w, 1, 1 - bit)

    def to_all(v):
        return [pair(cell(v, 0, (me // 4) ^ m), 4 * m) for m in range(1, others)]

    def heads_of(s, first):
        return attend(number[s], first, kt, vt, dot, rq, rk, vrow, qg, kg, heads, hdim, slots)

    left, qt, kt, vt, dot, rq, rk, right = project(x, dz, lng, win, wout, qgs, kg, heads, hdim)
    half = quarter // 2
    o0, dq0, dk0, dv0, gq0, gk0 = heads_of(0, gate(qt, *a, gains))
    b = [[across(gate(piece_b[:half], a[0]))]]
    a.append(pair(a[0], 2))
    cuts = (0, slots)
    n0 = back_rows(number[0], gate(dq0, a[1], *b[0]), dk0, dv0, right, win, cuts)
    b[0].append(across(gate(piece_b[half:], dq0)))
    a += [pair(gate(v, dq0), 1) for v in a]
    b.append([pair(b[0][0], 4)])
    f0 = [across(gate(n0[0], b[0][1]))]
    early = early_grads(gate(left, *n0), right)
    early = gate(early, b[0][1], b[1][0])
    early_rs = lax.psum_scatter(early, "dp", scatter_dimension=0, tiled=True)
    b[1].append(pair(b[0][1], 4))
    o1, dq1, dk1, dv1, gq1, gk1 = heads_of(1, gate(qt, early))
    n1 = back_rows(number[1], gate(dq1, b[1][1], *a), dk1, dv1, right, win, (0, slots))
    b += [[pair(gate(v, dq1), 1) for v in part] for part in b]
    small = small_terms((gq0 + gq1).reshape(heads, hdim), (gk0 + gk1).reshape(heads, hdim), width, shards)
    core = (me % 2).astype(jnp.int32).reshape(1)
    keep, send = late_grads(core, gate(left, *n1), [o0, o1], [dq0, dq1], [dk0, dk1], [dv0, dv1], small, low)
    send = gate(send, *b[2], *b[3], f0[0])
    f1 = [across(gate(v, send)) for v in n1]
    got = pair(send, 1)
    wb = unpack(mine_b, [(gate(b[0][0], send), b[0][1])] + b[1:])
    keep, send = by_two(keep, gate(got, wb))
    got = pair(send, 2)
    gains = gains.reshape(-1, 1)
    qf, kf, vf, wa, *blank = heads_fwd(mine_a, gate(gains[:inner], send), gains[inner:], left, a, heads, hdim)
    of = attend_fwd(qf, kf, vf, vrow, heads, hdim, slots)
    keep = keep + gate(got, of)
    got = to_all(keep)
    outs = out_rows(number[0], gate(x, keep), dz, lng, wout, wa, wb, o0, right, of, n0, f0, cuts, blank)
    late_rs = cell(keep, 0, me // 4) + sum(gate(v, outs[0]) for v in got)
    bo, d_in = out_rows(number[1], gate(x, outs[0], *f1), dz, lng, wout, wa, wb, o1, right, of, n1, f1, (0, slots), outs)
    block_output = bo.reshape(patches.shape)
    d_in = d_in.reshape(patches.shape)
    g_w_out = jnp.concatenate([late_rs[:, :inner], early_rs[:, :hidden]], axis=1).T[None]
    g_w_in = jnp.concatenate([late_rs[:, inner : 4 * inner], early_rs[:, hidden:]], axis=1)[None]
    band = lambda v: lax.dynamic_slice_in_dim(v, me * (width // shards), width // shards, 0)
    g_ln = jnp.sum(band(win).astype(F32) * g_w_in[0], axis=1) / band(ln_gain)
    g_ln = g_ln + across(g_ln)
    terms = late_rs[:, 4 * inner]
    count = inner // shards
    g_q = terms[:count].reshape(heads, hdim // shards)
    g_k = terms[count : 2 * count].reshape(heads, hdim // shards)
    return block_output, d_in, g_ln, g_w_in, g_q, g_k, g_w_out


def solution(mesh):
    placed = (
        P("dp", None, None),
        P("dp", None),
        P("dp"),
        P(),
        P("head", None, None),
        P("head", None),
        P("head", None),
        P("head", None, None),
        P("dp", None, None),
    )
    return jax.shard_map(
        functools.partial(per_device, mesh.shape["dp"]),
        mesh=mesh,
        in_specs=placed,
        out_specs=(
            P("dp", None, None),
            P("dp", None, None),
            P("dp"),
            P("head", "dp", None),
            P("head", "dp"),
            P("head", "dp"),
            P("head", None, "dp"),
        ),
        check_vma=False,
    )
```

```python
import functools
import math

import jax
import jax.numpy as jnp
from jax import lax
from jax.experimental import pallas as pl
from jax.experimental.pallas import tpu as pltpu
from jax.sharding import PartitionSpec as P

EPS = 1e-06
LOG2E = 1.4426950408889634
F32 = jnp.float32
BF16 = jnp.bfloat16
VMEM = 67000000
COST = 560
BQ = 512
UNROLL = 1
NT = (((1,), (1,)), ((), ()))
NN = (((1,), (0,)), ((), ()))


def cost(us):
    return pl.CostEstimate(flops=int(us * COST * 1e6), bytes_accessed=1, transcendentals=0)


def mm(a, b, dims=NN):
    return lax.dot_general(a, b, dims, preferred_element_type=F32)


def gelu_parts(u):
    cdf = 0.5 + 0.5 * lax.erf(u * math.sqrt(0.5))
    return u * cdf, cdf + u * (jnp.exp2(u * u * (-0.5 * LOG2E)) * (1.0 / math.sqrt(2.0 * math.pi)))


def head_norm(v, gain, heads, hdim):
    tokens = v.shape[-1]
    v = v.reshape(heads, hdim, tokens)
    centre = v - jnp.mean(v, axis=1, keepdims=True)
    r = lax.rsqrt(jnp.mean(centre * centre, axis=1, keepdims=True) + EPS)
    n = (centre * r).reshape(heads * hdim, tokens)
    return (n * gain).astype(BF16), r


def layer_norm(x_ref, lng_ref):
    x = x_ref[...].astype(F32)
    centre = x - jnp.mean(x, axis=-1, keepdims=True)
    r = lax.rsqrt(jnp.mean(centre * centre, axis=-1, keepdims=True) + EPS)
    return (centre * r * lng_ref[...]).astype(BF16)


def project_kernel(heads, hdim, first_ref, x_ref, dz_ref, lng_ref, win_ref, wout_ref, qg_ref, kg_ref,
                   left_ref, qt_ref, kt_ref, vt_ref, dot_ref, rq_ref, rk_ref, right_ref, wt_ref, xn_ref):
    inner = heads * hdim
    now = lax.rem(pl.program_id(0), 2)

    @pl.when(pl.program_id(0) == 0)
    def _():
        wt_ref[...] = win_ref[:, : 3 * inner].T
        xn_ref[0] = layer_norm(first_ref, lng_ref)

    xn = xn_ref[now]
    xn_ref[1 - now] = layer_norm(x_ref, lng_ref)
    dz = dz_ref[...]
    width = dz.shape[1]
    left_ref[:width, :] = dz.T
    left_ref[width:, :] = xn.T
    qkv = mm(wt_ref[...], xn, NT)
    qn, rq = head_norm(qkv[:inner], qg_ref[...], heads, hdim)
    kn, rk = head_norm(qkv[inner : 2 * inner], kg_ref[...], heads, hdim)
    qt_ref[...] = qn
    kt_ref[...] = kn
    rq_ref[...] = rq
    rk_ref[...] = rk
    vt_ref[...] = qkv[2 * inner :].astype(BF16)
    dot_ref[...] = mm(wout_ref[:inner, :], dz, NT).astype(BF16)
    hidden = win_ref.shape[1] - 3 * inner
    step = 512
    for c in range(0, hidden, step):
        u = mm(xn, win_ref[:, 3 * inner + c : 3 * inner + c + step])
        dh = mm(dz, wout_ref[inner + c : inner + c + step, :], NT)
        h, slope = gelu_parts(u)
        right_ref[:, c : c + step] = h.astype(BF16)
        right_ref[:, hidden + c : hidden + c + step] = (dh * slope).astype(BF16)


def project(x, dz, lng, win, wout, qg, kg, heads, hdim, tm=256):
    tokens, width = x.shape
    inner = heads * hdim
    gw = win.shape[1]
    hidden = gw - 3 * inner
    steps = tokens // tm
    given = lambda f: pl.BlockSpec((tm, width), lambda i: (f(i), 0))
    col = lambda n: pl.BlockSpec((n, tm), lambda i: (0, i))
    whole = lambda a: pl.BlockSpec(a.shape, lambda i: (0,) * a.ndim, pipeline_mode=pl.Buffered(1))
    stat = pl.BlockSpec((heads, 1, tm), lambda i: (0, 0, i))
    sds = jax.ShapeDtypeStruct
    return pl.pallas_call(
        functools.partial(project_kernel, heads, hdim),
        grid=(steps,),
        in_specs=[given(lambda i: 0), given(lambda i: jnp.minimum(i + 1, steps - 1)), given(lambda i: i), whole(lng), whole(win), whole(wout), whole(qg), whole(kg)],
        out_specs=[col(2 * width), col(inner), col(inner), col(inner), col(inner), stat, stat, pl.BlockSpec((tm, 2 * hidden), lambda i: (i, 0))],
        out_shape=[sds((2 * width, tokens), BF16)]
        + [sds((inner, tokens), BF16)] * 4
        + [sds((heads, 1, tokens), F32)] * 2
        + [sds((tokens, 2 * hidden), BF16)],
        scratch_shapes=[pltpu.VMEM((3 * inner, width), BF16), pltpu.VMEM((2, tm, width), BF16)],
        compiler_params=pltpu.CompilerParams(vmem_limit_bytes=VMEM),
        cost_estimate=cost(28),
        name="project",
    )(x, x, dz, lng, win, wout, qg, kg)


def attend_kernel(hdim, bq, nh, image_ref, qt_ref, kt_ref, vt_ref, dot_ref, rq_ref, rk_ref, vrow_ref, qg_ref, kg_ref,
                  o_ref, dq_ref, dk_ref, dv_ref, gq_ref, gk_ref, dqt_s, dkt_s, dvt_s, ot_s, kn_s, ktv_s, vs_s, va_s):
    tokens = qt_ref.shape[1]
    vrow = vrow_ref[0]
    vrow_b = vrow.astype(BF16)
    scale = hdim ** (-0.5)
    sub = lax.broadcasted_iota(jnp.int32, (16, tokens), 0)
    ones_row = jnp.where(sub == 0, jnp.broadcast_to(vrow, (16, tokens)), 0.0).astype(BF16)
    minus_row = jnp.where(sub < 2, 1.0, 0.0).astype(BF16)
    ktv_s[...] = kt_ref[...] * vrow_b
    for h in range(nh):
        rows = slice(h * hdim, (h + 1) * hdim)
        vt = vt_ref[rows, :]
        kn_s[h] = kt_ref[rows, :].T
        vs_s[h, :hdim, :] = vt * vrow_b
        vs_s[h, hdim:, :] = ones_row
        va_s[h] = jnp.concatenate([vt, minus_row], axis=0).T
    dkt_s[...] = jnp.zeros_like(dkt_s)
    dvt_s[...] = jnp.zeros_like(dvt_s)
    sub16 = lax.broadcasted_iota(jnp.int32, (16, bq), 0)

    def first(h, i):
        rows = slice(h * hdim, (h + 1) * hdim)
        at = pl.ds(pl.multiple_of(i * bq, bq), bq)
        return jnp.exp2(mm(kn_s[h], qt_ref[rows, at])).astype(BF16)

    def second(h, i, e):
        rows = slice(h * hdim, (h + 1) * hdim)
        at = pl.ds(pl.multiple_of(i * bq, bq), bq)
        qb = qt_ref[rows, at]
        dob = dot_ref[rows, at]
        oa = mm(vs_s[h], e)
        linv = 1.0 / oa[hdim : hdim + 1, :]
        o = oa[:hdim, :] * linv
        ot_s[rows, at] = o.astype(BF16)
        dof = dob.astype(F32)
        delta = jnp.sum(dof * o, axis=0, keepdims=True) * linv
        hi = delta.astype(BF16)
        lo = (delta - hi.astype(F32)).astype(BF16)
        dos = (dof * linv).astype(BF16)
        minus = jnp.where(sub16 == 0, -hi.astype(F32), jnp.where(sub16 == 1, -lo.astype(F32), 0.0)).astype(BF16)
        t = mm(va_s[h], jnp.concatenate([dos, minus], axis=0))
        ds = (e.astype(F32) * t).astype(BF16)
        dvt_s[rows, :] += mm(dos, e, NT)
        dkt_s[rows, :] += mm(qb, ds, NT)
        dqt_s[rows, at] = mm(ktv_s[rows, :], ds)

    def block(i, _):
        es = [first(h, i) for h in range(nh)]
        for h in range(nh):
            second(h, i, es[h])
        return 0

    lax.fori_loop(0, tokens // bq, block, 0, unroll=UNROLL)

    for p in range(nh // 2):
        prow = slice(p * 2 * hdim, (p + 1) * 2 * hdim)
        o_ref[:, prow] = ot_s[prow, :].T
        dv_ref[:, prow] = (dvt_s[prow, :] * vrow).astype(BF16).T
        for src, raw, r_ref, g_ref, grad_ref, dst, mul, c in (
            (dqt_s, qt_ref, rq_ref, qg_ref, gq_ref, dq_ref, scale, scale * LOG2E),
            (dkt_s, kt_ref, rk_ref, kg_ref, gk_ref, dk_ref, 1.0 / LOG2E, 1.0),
        ):
            both = []
            for h in (2 * p, 2 * p + 1):
                rows = slice(h * hdim, (h + 1) * hdim)
                g = g_ref[rows, :]
                inv = 1.0 / (g * c)
                d = src[rows, :]
                if raw is kt_ref:
                    d = d * vrow
                x = raw[rows, :].astype(F32)
                prod = d * x
                grad_ref[rows, :] = jnp.sum(prod, axis=1, keepdims=True) * (inv * mul)
                a = d * (g * mul)
                m1 = jnp.mean(a, axis=0, keepdims=True)
                m2 = jnp.mean(prod, axis=0, keepdims=True) * (mul / c)
                both.append((r_ref[h] * (a - m1 - (x * inv) * m2)).astype(BF16))
            dst[:, prow] = jnp.concatenate(both, axis=0).T

def attend(image, qt, kt, vt, dot, rq, rk, vrow, qg, kg, heads, hdim, slots, bq=BQ, nh=2):
    inner = heads * hdim
    w = nh * hdim
    sds = jax.ShapeDtypeStruct
    tcol = pl.BlockSpec((w, slots), lambda p, im: (p, im[0]))
    stat = pl.BlockSpec((nh, 1, slots), lambda p, im: (p, 0, im[0]))
    gain = pl.BlockSpec((w, 1), lambda p, im: (p, 0))
    row = pl.BlockSpec((slots, w), lambda p, im: (0, p))
    return pl.pallas_call(
        functools.partial(attend_kernel, hdim, min(bq, slots), nh),
        grid_spec=pltpu.PrefetchScalarGridSpec(
            num_scalar_prefetch=1,
            grid=(heads // nh,),
            in_specs=[tcol, tcol, tcol, tcol, stat, stat, pl.BlockSpec((1, 1, slots), lambda p, im: (im[0], 0, 0)), gain, gain],
            out_specs=[row, row, row, row, gain, gain],
            scratch_shapes=[pltpu.VMEM((w, slots), F32)] * 3
            + [
                pltpu.VMEM((w, slots), BF16),
                pltpu.VMEM((nh, slots, hdim), BF16),
                pltpu.VMEM((w, slots), BF16),
                pltpu.VMEM((nh, hdim + 16, slots), BF16),
                pltpu.VMEM((nh, slots, hdim + 16), BF16),
            ],
        ),
        out_shape=[sds((slots, inner), BF16)] * 4 + [sds((inner, 1), F32)] * 2,
        compiler_params=pltpu.CompilerParams(vmem_limit_bytes=VMEM),
        cost_estimate=cost(25),
        name="attend",
    )(image, qt, kt, vt, dot, rq, rk, vrow, qg, kg)


def overlaps(cuts, step, tm):
    for k in range(len(cuts) - 1):
        low, high = max(step * tm, cuts[k]), min((step + 1) * tm, cuts[k + 1])
        if low < high:
            yield k, low - cuts[k], low - step * tm, high - low


def back_rows_kernel(inner, cuts, steps, image_ref, dq_ref, dk_ref, dv_ref, du_ref, w_ref, *outs):
    g = (
        mm(dq_ref[...], w_ref[:, :inner], NT)
        + mm(dk_ref[...], w_ref[:, inner : 2 * inner], NT)
        + mm(dv_ref[...], w_ref[:, 2 * inner : 3 * inner], NT)
        + mm(du_ref[...], w_ref[:, 3 * inner :], NT)
    )
    if len(outs) == 1:
        outs[0][...] = g
        return
    for step in range(steps):

        @pl.when(pl.program_id(0) == step)
        def _(step=step):
            for k, at, low, n in overlaps(cuts, step, g.shape[0]):
                outs[k][at : at + n, :] = g[low : low + n]


def back_rows(image, dq, dk, dv, right, win, cuts, tm=256):
    slots, inner = dq.shape
    width, gw = win.shape
    hidden = gw - 3 * inner
    steps = slots // tm
    row = lambda n: pl.BlockSpec((tm, n), lambda i, im: (i, 0))
    parts = [b - a for a, b in zip(cuts, cuts[1:])]
    return pl.pallas_call(
        functools.partial(back_rows_kernel, inner, cuts, steps),
        grid_spec=pltpu.PrefetchScalarGridSpec(
            num_scalar_prefetch=1,
            grid=(steps,),
            in_specs=[row(inner)] * 3 + [pl.BlockSpec((tm, hidden), lambda i, im: (im[0] * steps + i, 1)), pl.BlockSpec(win.shape, lambda i, im: (0, 0), pipeline_mode=pl.Buffered(1))],
            out_specs=[pl.BlockSpec((n, width), lambda i, im: (0, 0)) for n in parts] if len(parts) > 1 else [row(width)],
        ),
        out_shape=[jax.ShapeDtypeStruct((n, width), F32) for n in parts],
        compiler_params=pltpu.CompilerParams(vmem_limit_bytes=VMEM),
        cost_estimate=cost(10),
        name="back_rows",
    )(image, dq, dk, dv, right, win)


def fetch(me, parts, stage, sem):
    rows = stage.shape[0] // len(parts)
    for k, refs in enumerate(parts):
        block = jnp.bitwise_xor(me, k)
        low = 0
        for ref in refs:
            pltpu.make_async_copy(ref, stage.at[pl.ds(pl.multiple_of(block * rows + low, 8), ref.shape[0])], sem.at[block]).start()
            low += ref.shape[0]


def grouped(counts, refs):
    out = []
    for n in counts:
        out.append(refs[:n])
        refs = refs[n:]
    return out


def arrived(block, rows, stage, sem):
    view = stage.at[pl.ds(pl.multiple_of(block * rows, 8), rows)]
    pltpu.make_async_copy(view, view, sem.at[block]).wait()


def unpack_kernel(counts, me_ref, *refs):
    parts, (out_ref, stage, sem) = grouped(counts, refs[:-3]), refs[-3:]
    step = pl.program_id(0)
    rows = out_ref.shape[0]

    @pl.when(step == 0)
    def _():
        fetch(me_ref[0], parts, stage, sem)

    arrived(step, rows, stage, sem)
    out_ref[...] = stage[pl.ds(pl.multiple_of(step * rows, 8), rows), :].astype(BF16)


def unpack(me, parts):
    pieces = len(parts)
    flat = [v for part in parts for v in part]
    rows, n = sum(v.shape[0] for v in parts[0]), flat[0].shape[1]
    return pl.pallas_call(
        functools.partial(unpack_kernel, tuple(len(part) for part in parts)),
        grid_spec=pltpu.PrefetchScalarGridSpec(
            num_scalar_prefetch=1,
            grid=(pieces,),
            in_specs=[pl.BlockSpec(memory_space=pl.ANY)] * len(flat),
            out_specs=pl.BlockSpec((rows, n), lambda i, me: (i, 0)),
            scratch_shapes=[pltpu.VMEM((rows * pieces, n), F32), pltpu.SemaphoreType.DMA((pieces,))],
        ),
        out_shape=jax.ShapeDtypeStruct((rows * pieces, n), BF16),
        compiler_params=pltpu.CompilerParams(vmem_limit_bytes=VMEM),
        cost_estimate=cost(6),
        name="unpack",
    )(me, *flat)


def heads_fwd_kernel(heads, hdim, me_ref, qg_ref, kg_ref, xnt_ref, *refs):
    parts, (qt_ref, kt_ref, vt_ref, wo_ref, _, _, wt_ref, stage, sem) = refs[:-9], refs[-9:]
    inner = heads * hdim

    @pl.when(pl.program_id(0) == 0)
    def _():
        fetch(me_ref[0], [(ref,) for ref in parts], stage, sem)
        for k in range(len(parts)):
            arrived(k, parts[0].shape[0], stage, sem)
        wt_ref[...] = stage[:, : 3 * inner].astype(BF16).T
        wo_ref[...] = stage[:, 3 * inner :].astype(BF16)

    qkv = mm(wt_ref[...], xnt_ref[...])
    qt_ref[...] = head_norm(qkv[:inner], qg_ref[...], heads, hdim)[0]
    kt_ref[...] = head_norm(qkv[inner : 2 * inner], kg_ref[...], heads, hdim)[0]
    vt_ref[...] = qkv[2 * inner :].astype(BF16)


def heads_fwd(me, qg, kg, left, parts, heads, hdim, tm=512):
    width, tokens = left.shape[0] // 2, left.shape[1]
    inner = heads * hdim
    n = parts[0].shape[1]
    col = pl.BlockSpec((inner, tm), lambda i, me: (0, i))
    gain = pl.BlockSpec((inner, 1), lambda i, me: (0, 0))
    out = pl.BlockSpec((width, inner), lambda i, me: (0, 0))
    raw = pl.BlockSpec(memory_space=pl.ANY)
    sds = jax.ShapeDtypeStruct
    return pl.pallas_call(
        functools.partial(heads_fwd_kernel, heads, hdim),
        grid_spec=pltpu.PrefetchScalarGridSpec(
            num_scalar_prefetch=1,
            grid=(tokens // tm,),
            in_specs=[gain, gain, pl.BlockSpec((width, tm), lambda i, me: (1, i))] + [raw] * len(parts),
            out_specs=[col, col, col, out, raw, raw],
            scratch_shapes=[pltpu.VMEM((3 * inner, width), BF16), pltpu.VMEM((width, n), F32), pltpu.SemaphoreType.DMA((len(parts),))],
        ),
        out_shape=[sds((inner, tokens), BF16)] * 3 + [sds((width, inner), BF16)] + [sds((tokens, width), BF16)] * 2,
        compiler_params=pltpu.CompilerParams(vmem_limit_bytes=VMEM),
        cost_estimate=cost(10),
        name="heads_fwd",
    )(me, qg, kg, left, *parts)


def attend_fwd_kernel(hdim, bq, nh, qt_ref, kt_ref, vt_ref, vrow_ref, o_ref, ot_s, kn_s, vs_s):
    tokens = qt_ref.shape[1]
    vrow = vrow_ref[0]
    vrow_b = vrow.astype(BF16)
    sub = lax.broadcasted_iota(jnp.int32, (16, tokens), 0)
    ones_row = jnp.where(sub == 0, jnp.broadcast_to(vrow, (16, tokens)), 0.0).astype(BF16)
    for h in range(nh):
        rows = slice(h * hdim, (h + 1) * hdim)
        kn_s[h] = kt_ref[rows, :].T
        vs_s[h, :hdim, :] = vt_ref[rows, :] * vrow_b
        vs_s[h, hdim:, :] = ones_row

    def block(i, _):
        at = pl.ds(pl.multiple_of(i * bq, bq), bq)
        es = [jnp.exp2(mm(kn_s[h], qt_ref[h * hdim : (h + 1) * hdim, at])).astype(BF16) for h in range(nh)]
        for h in range(nh):
            oa = mm(vs_s[h], es[h])
            ot_s[h * hdim : (h + 1) * hdim, at] = (oa[:hdim, :] * (1.0 / oa[hdim : hdim + 1, :])).astype(BF16)
        return 0

    lax.fori_loop(0, tokens // bq, block, 0, unroll=True)
    o_ref[...] = ot_s[...].T


def attend_fwd(qt, kt, vt, vrow, heads, hdim, slots, bq=BQ, nh=2):
    inner = heads * hdim
    w = nh * hdim
    seqs = qt.shape[1] // slots
    tcol = pl.BlockSpec((w, slots), lambda s, p: (p, s))
    return pl.pallas_call(
        functools.partial(attend_fwd_kernel, hdim, min(bq, slots), nh),
        grid=(seqs, heads // nh),
        in_specs=[tcol, tcol, tcol, pl.BlockSpec((1, 1, slots), lambda s, p: (s, 0, 0))],
        out_specs=pl.BlockSpec((slots, w), lambda s, p: (s, p)),
        out_shape=jax.ShapeDtypeStruct((seqs * slots, inner), BF16),
        scratch_shapes=[pltpu.VMEM((w, slots), BF16), pltpu.VMEM((nh, slots, hdim), BF16), pltpu.VMEM((nh, hdim + 16, slots), BF16)],
        compiler_params=pltpu.CompilerParams(vmem_limit_bytes=VMEM),
        cost_estimate=cost(16),
        name="attend_fwd",
    )(qt, kt, vt, vrow)


def out_rows_kernel(inner, cuts, steps, image_ref, x_ref, dz_ref, lng_ref, w_ref, wa_ref, wb_ref, o_ref, hid_ref, of_ref, *refs):
    pieces = len(cuts) - 1
    near, far = refs[:pieces], refs[pieces : 2 * pieces]
    out_ref, din_ref, both, sem = refs[-4:]
    tm = x_ref.shape[0]
    now = pl.program_id(0)

    @pl.when(now == 0)
    def _():
        for step in range(steps):
            for k, at, low, n in overlaps(cuts, step, tm):
                for side, parts in enumerate((near, far)):
                    pltpu.make_async_copy(parts[k].at[pl.ds(at, n)], both.at[step, side, pl.ds(low, n)], sem.at[step]).start()

    x = x_ref[...].astype(F32)
    centre = x - jnp.mean(x, axis=-1, keepdims=True)
    r = lax.rsqrt(jnp.mean(centre * centre, axis=-1, keepdims=True) + EPS)
    n = centre * r
    scaled = n * lng_ref[...]
    xn = scaled.astype(BF16)
    hidden = wb_ref.shape[1] // 2
    total = mm(o_ref[...], w_ref[:inner, :]) + mm(hid_ref[...], w_ref[inner:, :]) + mm(of_ref[...], wa_ref[...], NT)
    parts = []
    for c in range(0, hidden, 512):
        parts.append(gelu_parts(mm(xn, wb_ref[:, c : c + 512]))[0].astype(BF16))
    total = total + mm(jnp.concatenate(parts, axis=1), wb_ref[:, hidden:], NT)
    out_ref[...] = (x + total).astype(BF16)
    pltpu.make_async_copy(both.at[now], both.at[now], sem.at[now]).wait()
    a = (both[now, 0] + both[now, 1]) * lng_ref[...]
    back = r * (a - jnp.mean(a, axis=-1, keepdims=True) - n * jnp.mean(a * n, axis=-1, keepdims=True))
    din_ref[...] = (dz_ref[...].astype(F32) + back).astype(BF16)


def out_rows(image, x, dz, lng, wout, wa, wb, o, right, of, near, far, cuts, prior, tm=256):
    slots, inner = o.shape
    go, width = wout.shape
    steps = slots // tm
    row = lambda n: pl.BlockSpec((tm, n), lambda i, im: (i, 0))
    of_image = lambda n: pl.BlockSpec((tm, n), lambda i, im: (im[0] * steps + i, 0))
    at = of_image(width)
    whole = lambda a: pl.BlockSpec(a.shape, lambda i, im: (0,) * a.ndim, pipeline_mode=pl.Buffered(1))
    given = [image, x, dz, lng, wout, wa, wb, o, right, of, *near, *far]
    raw = pl.BlockSpec(memory_space=pl.ANY)
    return pl.pallas_call(
        functools.partial(out_rows_kernel, inner, cuts, steps),
        grid_spec=pltpu.PrefetchScalarGridSpec(
            num_scalar_prefetch=1,
            grid=(steps,),
            in_specs=[at, at, whole(lng), whole(wout), whole(wa), whole(wb), row(inner), of_image(go - inner), of_image(inner)] + [raw] * (len(near) + len(far) + 2),
            out_specs=[at, at],
            scratch_shapes=[pltpu.VMEM((steps, 2, tm, width), F32), pltpu.SemaphoreType.DMA((steps,))],
        ),
        out_shape=[jax.ShapeDtypeStruct(x.shape, BF16)] * 2,
        input_output_aliases={len(given) + k: k for k in range(2)},
        compiler_params=pltpu.CompilerParams(vmem_limit_bytes=VMEM),
        cost_estimate=cost(18),
        name="out_rows",
    )(*given, *prior)


def early_kernel(left_ref, right_ref, out_ref):
    out_ref[...] = mm(left_ref[...], right_ref[...])


def early_grads(left, right, tn=512):
    width, tokens = left.shape[0] // 2, left.shape[1]
    both = right.shape[1]
    steps = both // tn
    return pl.pallas_call(
        early_kernel,
        grid=(steps,),
        in_specs=[pl.BlockSpec((width, tokens), lambda j: (jnp.where(j < steps // 2, 0, 1), 0)), pl.BlockSpec((tokens, tn), lambda j: (0, j))],
        out_specs=pl.BlockSpec((width, tn), lambda j: (0, j)),
        out_shape=jax.ShapeDtypeStruct((width, both), F32),
        compiler_params=pltpu.CompilerParams(vmem_limit_bytes=VMEM),
        cost_estimate=cost(16),
        name="early_grads",
    )(left, right)


def late_kernel(seqs, low, core_ref, *refs):
    dzt, xnt = refs[:seqs], refs[seqs : 2 * seqs]
    o, dq, dk, dv = (refs[(2 + k) * seqs : (3 + k) * seqs] for k in range(4))
    small, keep, send = refs[-3:]
    width = o[0].shape[1]

    def store(cols, v):
        for half in range(2):
            rows = jnp.concatenate([v[b : b + low] for b in range(half * low, v.shape[0], 2 * low)], axis=0)

            @pl.when(core_ref[0] == half)
            def _():
                keep[:, cols] = rows

            @pl.when(core_ref[0] != half)
            def _():
                send[:, cols] = rows

    for k, (left, right) in enumerate(((dzt, o), (xnt, dq), (xnt, dk), (xnt, dv))):
        store(slice(k * width, (k + 1) * width), sum(mm(left[s][...], right[s][...]) for s in range(seqs)))
    store(slice(4 * width, 4 * width + 128), jnp.broadcast_to(small[...], (small.shape[0], 128)))


def late_grads(core, left, o, dq, dk, dv, small, low):
    seqs = len(o)
    slots, inner = o[0].shape
    width = left.shape[0] // 2
    tm = 4 * low
    while tm < 192:
        tm *= 2
    steps = width // tm
    above = [pl.BlockSpec((tm, slots), lambda i, c, s=s: (i, s)) for s in range(seqs)]
    below = [pl.BlockSpec((tm, slots), lambda i, c, s=s: (steps + i, s)) for s in range(seqs)]
    whole = pl.BlockSpec((slots, inner), lambda i, c: (0, 0), pipeline_mode=pl.Buffered(1))
    wide = 4 * inner + 128
    out = pl.BlockSpec((tm // 2, wide), lambda i, c: (i, 0))
    return pl.pallas_call(
        functools.partial(late_kernel, seqs, low),
        grid_spec=pltpu.PrefetchScalarGridSpec(
            num_scalar_prefetch=1,
            grid=(steps,),
            in_specs=above + below + [whole] * (4 * seqs) + [pl.BlockSpec((tm, 1), lambda i, c: (i, 0))],
            out_specs=[out, out],
        ),
        out_shape=[jax.ShapeDtypeStruct((width // 2, wide), F32)] * 2,
        compiler_params=pltpu.CompilerParams(vmem_limit_bytes=VMEM),
        cost_estimate=cost(12),
        name="late_grads",
    )(core, *[left] * (2 * seqs), *o, *dq, *dk, *dv, small)


def gate(value, *done):
    return lax.optimization_barrier((value, *done))[0]


def per_device(shards, patches, keep_mask, counts, ln_gain, w_in, q_gain, k_gain, w_out, d_out):
    seqs, slots, width = patches.shape
    heads, hdim = q_gain.shape
    inner = heads * hdim
    swap = [(0, 1), (1, 0)]
    scale = hdim ** (-0.5)
    win, wout = w_in[0], w_out[0]
    hidden = wout.shape[0] - inner
    x = patches.reshape(seqs * slots, width)
    dz = d_out.reshape(seqs * slots, width)
    slot_ids = jnp.arange(slots, dtype=jnp.int32)
    valid = (slot_ids[None, :] < counts[:, None]) & ((keep_mask == 1) | (slot_ids[None, :] == 0))
    vrow = valid.astype(F32).reshape(seqs, 1, slots)
    qg = q_gain.reshape(inner, 1)
    kg = k_gain.reshape(inner, 1)
    lng = ln_gain.reshape(1, width)
    qgs = qg * (scale * LOG2E)
    across = lambda v: lax.ppermute(v, "head", swap)

    def pair(v, bit):
        return lax.ppermute(v, "dp", [(i, i ^ bit) for i in range(shards)])

    number = [jnp.full((1,), s, jnp.int32) for s in range(seqs)]
    me = lax.axis_index("dp")

    quarter = width // 4

    def rows_of(bit, left_cols, right_rows):
        mine = ((me // bit) % 2) + 2 * (me % 2)
        rows = lax.dynamic_slice(win, (mine * quarter, left_cols[0]), (quarter, left_cols[1] - left_cols[0]))
        cols = lax.dynamic_slice(wout, (right_rows[0], mine * quarter), (right_rows[1] - right_rows[0], quarter))
        return mine.astype(jnp.int32).reshape(1), jnp.concatenate([rows.astype(F32), cols.astype(F32).T], axis=1)

    mine_a, piece_a = rows_of(2, (0, 3 * inner), (0, inner))
    mine_b, piece_b = rows_of(4, (3 * inner, win.shape[1]), (inner, wout.shape[0]))
    gains = across(jnp.concatenate([qgs, kg], axis=0).reshape(-1, 128))
    split = quarter * 7 // 12
    b = [[across(piece_b[:split])]]

    low = width // shards
    cell = lambda v, axis, at: lax.dynamic_index_in_dim(v, at, axis, False)
    others = shards // 4

    def by_two(v, w):
        bit = (me // 2) % 2
        v, w = (u.reshape(others, 2, low, -1) for u in (v, w))
        return cell(v, 1, bit) + cell(w, 1, bit), cell(v, 1, 1 - bit) + cell(w, 1, 1 - bit)

    def to_all(v):
        return [pair(cell(v, 0, (me // 4) ^ m), 4 * m) for m in range(1, others)]

    def heads_of(s, first):
        return attend(number[s], first, kt, vt, dot, rq, rk, vrow, qg, kg, heads, hdim, slots)

    left, qt, kt, vt, dot, rq, rk, right = project(x, dz, lng, win, wout, qgs, kg, heads, hdim)
    o0, dq0, dk0, dv0, gq0, gk0 = heads_of(0, gate(qt, *b[0], gains))
    a = [across(gate(piece_a, *b[0]))]
    b.append([pair(b[0][0], 4)])
    cuts = (0, slots // 8, slots)
    n0 = back_rows(number[0], gate(dq0, *a), dk0, dv0, right, win, cuts)
    b[0].append(across(gate(piece_b[split:], *a)))
    a.append(pair(a[0], 2))
    f0 = [across(v) for v in n0]
    early = early_grads(gate(left, *n0), right)
    early = gate(early, b[0][1], b[1][0], a[1], f0[0])
    early_rs = lax.psum_scatter(early, "dp", scatter_dimension=0, tiled=True)
    b[1].append(pair(b[0][1], 4))
    o1, dq1, dk1, dv1, gq1, gk1 = heads_of(1, gate(qt, early))
    n1 = back_rows(number[1], gate(dq1, b[1][1]), dk1, dv1, right, win, (0, slots))
    a += [pair(gate(v, dq1), 1) for v in a]
    b += [[pair(gate(v, dq1), 1) for v in part] for part in b]
    part = lambda v: v.reshape(heads, shards, hdim // shards).transpose(1, 0, 2).reshape(shards, -1)
    small = jnp.concatenate([part(gq0 + gq1), part(gk0 + gk1)], axis=1)
    small = jnp.pad(small, ((0, 0), (0, low - small.shape[1]))).reshape(width, 1)
    core = (me % 2).astype(jnp.int32).reshape(1)
    keep, send = late_grads(core, gate(left, *n1), [o0, o1], [dq0, dq1], [dk0, dk1], [dv0, dv1], small, low)
    send = gate(send, *a, *b[2], *b[3], f0[1])
    f1 = [across(gate(v, send)) for v in n1]
    got = pair(send, 1)
    keep, send = by_two(keep, got)
    got = pair(send, 2)
    wb = unpack(mine_b, [(gate(b[0][0], send), b[0][1])] + b[1:])
    gains = gains.reshape(-1, 1)
    qf, kf, vf, wa, *blank = heads_fwd(mine_a, gate(gains[:inner], wb), gains[inner:], left, a, heads, hdim)
    of = attend_fwd(qf, kf, vf, vrow, heads, hdim, slots)
    keep = keep + gate(got, of)
    got = to_all(keep)
    outs = out_rows(number[0], gate(x, keep), dz, lng, wout, wa, wb, o0, right, of, n0, f0, cuts, blank)
    late_rs = cell(keep, 0, me // 4) + sum(got)
    g_w_out = jnp.concatenate([late_rs[:, :inner], early_rs[:, :hidden]], axis=1).T[None]
    g_w_in = jnp.concatenate([late_rs[:, inner : 4 * inner], early_rs[:, hidden:]], axis=1)[None]
    band = lambda v: lax.dynamic_slice_in_dim(v, me * (width // shards), width // shards, 0)
    g_ln = jnp.sum(band(win).astype(F32) * g_w_in[0], axis=1) / band(ln_gain)
    bo, d_in = out_rows(number[1], gate(x, outs[0], *f1), dz, lng, wout, wa, wb, o1, right, of, n1, f1, (0, slots), outs)
    block_output = bo.reshape(patches.shape)
    d_in = d_in.reshape(patches.shape)
    g_ln = g_ln + across(g_ln)
    terms = late_rs[:, 4 * inner]
    count = inner // shards
    g_q = terms[:count].reshape(heads, hdim // shards)
    g_k = terms[count : 2 * count].reshape(heads, hdim // shards)
    return block_output, d_in, g_ln, g_w_in, g_q, g_k, g_w_out


def solution(mesh):
    placed = (
        P("dp", None, None),
        P("dp", None),
        P("dp"),
        P(),
        P("head", None, None),
        P("head", None),
        P("head", None),
        P("head", None, None),
        P("dp", None, None),
    )
    return jax.shard_map(
        functools.partial(per_device, mesh.shape["dp"]),
        mesh=mesh,
        in_specs=placed,
        out_specs=(
            P("dp", None, None),
            P("dp", None, None),
            P("dp"),
            P("head", "dp", None),
            P("head", "dp"),
            P("head", "dp"),
            P("head", None, "dp"),
        ),
        check_vma=False,
    )
```

```python
import functools
import math

import jax
import jax.numpy as jnp
from jax import lax
from jax.experimental import pallas as pl
from jax.experimental.pallas import tpu as pltpu
from jax.sharding import PartitionSpec as P

EPS = 1e-06
LOG2E = 1.4426950408889634
F32 = jnp.float32
BF16 = jnp.bfloat16
VMEM = 67000000
COST = 560
BQ = 512
UNROLL = 1
NT = (((1,), (1,)), ((), ()))
NN = (((1,), (0,)), ((), ()))


def cost(us):
    return pl.CostEstimate(flops=int(us * COST * 1e6), bytes_accessed=1, transcendentals=0)


def mm(a, b, dims=NN):
    return lax.dot_general(a, b, dims, preferred_element_type=F32)


def gelu_parts(u):
    cdf = 0.5 + 0.5 * lax.erf(u * math.sqrt(0.5))
    return u * cdf, cdf + u * (jnp.exp2(u * u * (-0.5 * LOG2E)) * (1.0 / math.sqrt(2.0 * math.pi)))


def head_norm(v, gain, heads, hdim):
    tokens = v.shape[-1]
    v = v.reshape(heads, hdim, tokens)
    centre = v - jnp.mean(v, axis=1, keepdims=True)
    r = lax.rsqrt(jnp.mean(centre * centre, axis=1, keepdims=True) + EPS)
    n = (centre * r).reshape(heads * hdim, tokens)
    return (n * gain).astype(BF16), r


def layer_norm(x_ref, lng_ref):
    x = x_ref[...].astype(F32)
    centre = x - jnp.mean(x, axis=-1, keepdims=True)
    r = lax.rsqrt(jnp.mean(centre * centre, axis=-1, keepdims=True) + EPS)
    return (centre * r * lng_ref[...]).astype(BF16)


def project_kernel(heads, hdim, first_ref, x_ref, dz_ref, lng_ref, win_ref, wout_ref, qg_ref, kg_ref,
                   left_ref, qt_ref, kt_ref, vt_ref, dot_ref, rq_ref, rk_ref, right_ref, wt_ref, xn_ref):
    inner = heads * hdim
    now = lax.rem(pl.program_id(0), 2)

    @pl.when(pl.program_id(0) == 0)
    def _():
        wt_ref[...] = win_ref[:, : 3 * inner].T
        xn_ref[0] = layer_norm(first_ref, lng_ref)

    xn = xn_ref[now]
    xn_ref[1 - now] = layer_norm(x_ref, lng_ref)
    dz = dz_ref[...]
    width = dz.shape[1]
    left_ref[:width, :] = dz.T
    left_ref[width:, :] = xn.T
    qkv = mm(wt_ref[...], xn, NT)
    qn, rq = head_norm(qkv[:inner], qg_ref[...], heads, hdim)
    kn, rk = head_norm(qkv[inner : 2 * inner], kg_ref[...], heads, hdim)
    qt_ref[...] = qn
    kt_ref[...] = kn
    rq_ref[...] = rq
    rk_ref[...] = rk
    vt_ref[...] = qkv[2 * inner :].astype(BF16)
    dot_ref[...] = mm(wout_ref[:inner, :], dz, NT).astype(BF16)
    hidden = win_ref.shape[1] - 3 * inner
    step = 512
    for c in range(0, hidden, step):
        u = mm(xn, win_ref[:, 3 * inner + c : 3 * inner + c + step])
        dh = mm(dz, wout_ref[inner + c : inner + c + step, :], NT)
        h, slope = gelu_parts(u)
        right_ref[:, c : c + step] = h.astype(BF16)
        right_ref[:, hidden + c : hidden + c + step] = (dh * slope).astype(BF16)


def project(x, dz, lng, win, wout, qg, kg, heads, hdim, tm=256):
    tokens, width = x.shape
    inner = heads * hdim
    gw = win.shape[1]
    hidden = gw - 3 * inner
    steps = tokens // tm
    given = lambda f: pl.BlockSpec((tm, width), lambda i: (f(i), 0))
    col = lambda n: pl.BlockSpec((n, tm), lambda i: (0, i))
    whole = lambda a: pl.BlockSpec(a.shape, lambda i: (0,) * a.ndim, pipeline_mode=pl.Buffered(1))
    stat = pl.BlockSpec((heads, 1, tm), lambda i: (0, 0, i))
    sds = jax.ShapeDtypeStruct
    return pl.pallas_call(
        functools.partial(project_kernel, heads, hdim),
        grid=(steps,),
        in_specs=[given(lambda i: 0), given(lambda i: jnp.minimum(i + 1, steps - 1)), given(lambda i: i), whole(lng), whole(win), whole(wout), whole(qg), whole(kg)],
        out_specs=[col(2 * width), col(inner), col(inner), col(inner), col(inner), stat, stat, pl.BlockSpec((tm, 2 * hidden), lambda i: (i, 0))],
        out_shape=[sds((2 * width, tokens), BF16)]
        + [sds((inner, tokens), BF16)] * 4
        + [sds((heads, 1, tokens), F32)] * 2
        + [sds((tokens, 2 * hidden), BF16)],
        scratch_shapes=[pltpu.VMEM((3 * inner, width), BF16), pltpu.VMEM((2, tm, width), BF16)],
        compiler_params=pltpu.CompilerParams(vmem_limit_bytes=VMEM),
        cost_estimate=cost(28),
        name="project",
    )(x, x, dz, lng, win, wout, qg, kg)


def attend_kernel(hdim, bq, nh, image_ref, qt_ref, kt_ref, vt_ref, dot_ref, rq_ref, rk_ref, vrow_ref, qg_ref, kg_ref,
                  o_ref, dq_ref, dk_ref, dv_ref, gq_ref, gk_ref, dqt_s, dkt_s, dvt_s, ot_s, kn_s, ktv_s, vs_s, va_s):
    tokens = qt_ref.shape[1]
    vrow = vrow_ref[0]
    vrow_b = vrow.astype(BF16)
    scale = hdim ** (-0.5)
    sub = lax.broadcasted_iota(jnp.int32, (16, tokens), 0)
    ones_row = jnp.where(sub == 0, jnp.broadcast_to(vrow, (16, tokens)), 0.0).astype(BF16)
    minus_row = jnp.where(sub < 2, 1.0, 0.0).astype(BF16)
    ktv_s[...] = kt_ref[...] * vrow_b
    for h in range(nh):
        rows = slice(h * hdim, (h + 1) * hdim)
        vt = vt_ref[rows, :]
        kn_s[h] = kt_ref[rows, :].T
        vs_s[h, :hdim, :] = vt * vrow_b
        vs_s[h, hdim:, :] = ones_row
        va_s[h] = jnp.concatenate([vt, minus_row], axis=0).T
    dkt_s[...] = jnp.zeros_like(dkt_s)
    dvt_s[...] = jnp.zeros_like(dvt_s)
    sub16 = lax.broadcasted_iota(jnp.int32, (16, bq), 0)

    def first(h, i):
        rows = slice(h * hdim, (h + 1) * hdim)
        at = pl.ds(pl.multiple_of(i * bq, bq), bq)
        return jnp.exp2(mm(kn_s[h], qt_ref[rows, at])).astype(BF16)

    def second(h, i, e):
        rows = slice(h * hdim, (h + 1) * hdim)
        at = pl.ds(pl.multiple_of(i * bq, bq), bq)
        qb = qt_ref[rows, at]
        dob = dot_ref[rows, at]
        oa = mm(vs_s[h], e)
        linv = 1.0 / oa[hdim : hdim + 1, :]
        o = oa[:hdim, :] * linv
        ot_s[rows, at] = o.astype(BF16)
        dof = dob.astype(F32)
        delta = jnp.sum(dof * o, axis=0, keepdims=True) * linv
        hi = delta.astype(BF16)
        lo = (delta - hi.astype(F32)).astype(BF16)
        dos = (dof * linv).astype(BF16)
        minus = jnp.where(sub16 == 0, -hi.astype(F32), jnp.where(sub16 == 1, -lo.astype(F32), 0.0)).astype(BF16)
        t = mm(va_s[h], jnp.concatenate([dos, minus], axis=0))
        ds = (e.astype(F32) * t).astype(BF16)
        dvt_s[rows, :] += mm(dos, e, NT)
        dkt_s[rows, :] += mm(qb, ds, NT)
        dqt_s[rows, at] = mm(ktv_s[rows, :], ds)

    def block(i, _):
        es = [first(h, i) for h in range(nh)]
        for h in range(nh):
            second(h, i, es[h])
        return 0

    lax.fori_loop(0, tokens // bq, block, 0, unroll=UNROLL)

    for p in range(nh // 2):
        prow = slice(p * 2 * hdim, (p + 1) * 2 * hdim)
        o_ref[:, prow] = ot_s[prow, :].T
        dv_ref[:, prow] = (dvt_s[prow, :] * vrow).astype(BF16).T
        for src, raw, r_ref, g_ref, grad_ref, dst, mul, c in (
            (dqt_s, qt_ref, rq_ref, qg_ref, gq_ref, dq_ref, scale, scale * LOG2E),
            (dkt_s, kt_ref, rk_ref, kg_ref, gk_ref, dk_ref, 1.0 / LOG2E, 1.0),
        ):
            both = []
            for h in (2 * p, 2 * p + 1):
                rows = slice(h * hdim, (h + 1) * hdim)
                g = g_ref[rows, :]
                inv = 1.0 / (g * c)
                d = src[rows, :]
                if raw is kt_ref:
                    d = d * vrow
                x = raw[rows, :].astype(F32)
                prod = d * x
                grad_ref[rows, :] = jnp.sum(prod, axis=1, keepdims=True) * (inv * mul)
                a = d * (g * mul)
                m1 = jnp.mean(a, axis=0, keepdims=True)
                m2 = jnp.mean(prod, axis=0, keepdims=True) * (mul / c)
                both.append((r_ref[h] * (a - m1 - (x * inv) * m2)).astype(BF16))
            dst[:, prow] = jnp.concatenate(both, axis=0).T

def attend(image, qt, kt, vt, dot, rq, rk, vrow, qg, kg, heads, hdim, slots, bq=BQ, nh=2):
    inner = heads * hdim
    w = nh * hdim
    sds = jax.ShapeDtypeStruct
    tcol = pl.BlockSpec((w, slots), lambda p, im: (p, im[0]))
    stat = pl.BlockSpec((nh, 1, slots), lambda p, im: (p, 0, im[0]))
    gain = pl.BlockSpec((w, 1), lambda p, im: (p, 0))
    row = pl.BlockSpec((slots, w), lambda p, im: (0, p))
    return pl.pallas_call(
        functools.partial(attend_kernel, hdim, min(bq, slots), nh),
        grid_spec=pltpu.PrefetchScalarGridSpec(
            num_scalar_prefetch=1,
            grid=(heads // nh,),
            in_specs=[tcol, tcol, tcol, tcol, stat, stat, pl.BlockSpec((1, 1, slots), lambda p, im: (im[0], 0, 0)), gain, gain],
            out_specs=[row, row, row, row, gain, gain],
            scratch_shapes=[pltpu.VMEM((w, slots), F32)] * 3
            + [
                pltpu.VMEM((w, slots), BF16),
                pltpu.VMEM((nh, slots, hdim), BF16),
                pltpu.VMEM((w, slots), BF16),
                pltpu.VMEM((nh, hdim + 16, slots), BF16),
                pltpu.VMEM((nh, slots, hdim + 16), BF16),
            ],
        ),
        out_shape=[sds((slots, inner), BF16)] * 4 + [sds((inner, 1), F32)] * 2,
        compiler_params=pltpu.CompilerParams(vmem_limit_bytes=VMEM),
        cost_estimate=cost(25),
        name="attend",
    )(image, qt, kt, vt, dot, rq, rk, vrow, qg, kg)


def overlaps(cuts, step, tm):
    for k in range(len(cuts) - 1):
        low, high = max(step * tm, cuts[k]), min((step + 1) * tm, cuts[k + 1])
        if low < high:
            yield k, low - cuts[k], low - step * tm, high - low


def back_rows_kernel(inner, cuts, steps, image_ref, dq_ref, dk_ref, dv_ref, du_ref, w_ref, *outs):
    g = (
        mm(dq_ref[...], w_ref[:, :inner], NT)
        + mm(dk_ref[...], w_ref[:, inner : 2 * inner], NT)
        + mm(dv_ref[...], w_ref[:, 2 * inner : 3 * inner], NT)
        + mm(du_ref[...], w_ref[:, 3 * inner :], NT)
    )
    if len(outs) == 1:
        outs[0][...] = g
        return
    for step in range(steps):

        @pl.when(pl.program_id(0) == step)
        def _(step=step):
            for k, at, low, n in overlaps(cuts, step, g.shape[0]):
                outs[k][at : at + n, :] = g[low : low + n]


def back_rows(image, dq, dk, dv, right, win, cuts, tm=256):
    slots, inner = dq.shape
    width, gw = win.shape
    hidden = gw - 3 * inner
    steps = slots // tm
    row = lambda n: pl.BlockSpec((tm, n), lambda i, im: (i, 0))
    parts = [b - a for a, b in zip(cuts, cuts[1:])]
    return pl.pallas_call(
        functools.partial(back_rows_kernel, inner, cuts, steps),
        grid_spec=pltpu.PrefetchScalarGridSpec(
            num_scalar_prefetch=1,
            grid=(steps,),
            in_specs=[row(inner)] * 3 + [pl.BlockSpec((tm, hidden), lambda i, im: (im[0] * steps + i, 1)), pl.BlockSpec(win.shape, lambda i, im: (0, 0), pipeline_mode=pl.Buffered(1))],
            out_specs=[pl.BlockSpec((n, width), lambda i, im: (0, 0)) for n in parts] if len(parts) > 1 else [row(width)],
        ),
        out_shape=[jax.ShapeDtypeStruct((n, width), F32) for n in parts],
        compiler_params=pltpu.CompilerParams(vmem_limit_bytes=VMEM),
        cost_estimate=cost(10),
        name="back_rows",
    )(image, dq, dk, dv, right, win)


def fetch(me, parts, stage, sem):
    rows = stage.shape[0] // len(parts)
    for k, refs in enumerate(parts):
        block = jnp.bitwise_xor(me, k)
        low = 0
        for ref in refs:
            pltpu.make_async_copy(ref, stage.at[pl.ds(pl.multiple_of(block * rows + low, 8), ref.shape[0])], sem.at[block]).start()
            low += ref.shape[0]


def grouped(counts, refs):
    out = []
    for n in counts:
        out.append(refs[:n])
        refs = refs[n:]
    return out


def arrived(block, rows, stage, sem):
    view = stage.at[pl.ds(pl.multiple_of(block * rows, 8), rows)]
    pltpu.make_async_copy(view, view, sem.at[block]).wait()


def unpack_kernel(counts, me_ref, *refs):
    parts, (out_ref, stage, sem) = grouped(counts, refs[:-3]), refs[-3:]
    step = pl.program_id(0)
    rows = out_ref.shape[0]

    @pl.when(step == 0)
    def _():
        fetch(me_ref[0], parts, stage, sem)

    arrived(step, rows, stage, sem)
    out_ref[...] = stage[pl.ds(pl.multiple_of(step * rows, 8), rows), :].astype(BF16)


def unpack(me, parts):
    pieces = len(parts)
    flat = [v for part in parts for v in part]
    rows, n = sum(v.shape[0] for v in parts[0]), flat[0].shape[1]
    return pl.pallas_call(
        functools.partial(unpack_kernel, tuple(len(part) for part in parts)),
        grid_spec=pltpu.PrefetchScalarGridSpec(
            num_scalar_prefetch=1,
            grid=(pieces,),
            in_specs=[pl.BlockSpec(memory_space=pl.ANY)] * len(flat),
            out_specs=pl.BlockSpec((rows, n), lambda i, me: (i, 0)),
            scratch_shapes=[pltpu.VMEM((rows * pieces, n), F32), pltpu.SemaphoreType.DMA((pieces,))],
        ),
        out_shape=jax.ShapeDtypeStruct((rows * pieces, n), BF16),
        compiler_params=pltpu.CompilerParams(vmem_limit_bytes=VMEM),
        cost_estimate=cost(6),
        name="unpack",
    )(me, *flat)


def heads_fwd_kernel(heads, hdim, me_ref, qg_ref, kg_ref, xnt_ref, *refs):
    parts, (qt_ref, kt_ref, vt_ref, wo_ref, _, _, wt_ref, stage, sem) = refs[:-9], refs[-9:]
    inner = heads * hdim

    @pl.when(pl.program_id(0) == 0)
    def _():
        fetch(me_ref[0], [(ref,) for ref in parts], stage, sem)
        for k in range(len(parts)):
            arrived(k, parts[0].shape[0], stage, sem)
        wt_ref[...] = stage[:, : 3 * inner].astype(BF16).T
        wo_ref[...] = stage[:, 3 * inner :].astype(BF16)

    qkv = mm(wt_ref[...], xnt_ref[...])
    qt_ref[...] = head_norm(qkv[:inner], qg_ref[...], heads, hdim)[0]
    kt_ref[...] = head_norm(qkv[inner : 2 * inner], kg_ref[...], heads, hdim)[0]
    vt_ref[...] = qkv[2 * inner :].astype(BF16)


def heads_fwd(me, qg, kg, left, parts, heads, hdim, tm=512):
    width, tokens = left.shape[0] // 2, left.shape[1]
    inner = heads * hdim
    n = parts[0].shape[1]
    col = pl.BlockSpec((inner, tm), lambda i, me: (0, i))
    gain = pl.BlockSpec((inner, 1), lambda i, me: (0, 0))
    out = pl.BlockSpec((width, inner), lambda i, me: (0, 0))
    raw = pl.BlockSpec(memory_space=pl.ANY)
    sds = jax.ShapeDtypeStruct
    return pl.pallas_call(
        functools.partial(heads_fwd_kernel, heads, hdim),
        grid_spec=pltpu.PrefetchScalarGridSpec(
            num_scalar_prefetch=1,
            grid=(tokens // tm,),
            in_specs=[gain, gain, pl.BlockSpec((width, tm), lambda i, me: (1, i))] + [raw] * len(parts),
            out_specs=[col, col, col, out, raw, raw],
            scratch_shapes=[pltpu.VMEM((3 * inner, width), BF16), pltpu.VMEM((width, n), F32), pltpu.SemaphoreType.DMA((len(parts),))],
        ),
        out_shape=[sds((inner, tokens), BF16)] * 3 + [sds((width, inner), BF16)] + [sds((tokens, width), BF16)] * 2,
        compiler_params=pltpu.CompilerParams(vmem_limit_bytes=VMEM),
        cost_estimate=cost(10),
        name="heads_fwd",
    )(me, qg, kg, left, *parts)


def attend_fwd_kernel(hdim, bq, nh, qt_ref, kt_ref, vt_ref, vrow_ref, o_ref, ot_s, kn_s, vs_s):
    tokens = qt_ref.shape[1]
    vrow = vrow_ref[0]
    vrow_b = vrow.astype(BF16)
    sub = lax.broadcasted_iota(jnp.int32, (16, tokens), 0)
    ones_row = jnp.where(sub == 0, jnp.broadcast_to(vrow, (16, tokens)), 0.0).astype(BF16)
    for h in range(nh):
        rows = slice(h * hdim, (h + 1) * hdim)
        kn_s[h] = kt_ref[rows, :].T
        vs_s[h, :hdim, :] = vt_ref[rows, :] * vrow_b
        vs_s[h, hdim:, :] = ones_row

    def block(i, _):
        at = pl.ds(pl.multiple_of(i * bq, bq), bq)
        es = [jnp.exp2(mm(kn_s[h], qt_ref[h * hdim : (h + 1) * hdim, at])).astype(BF16) for h in range(nh)]
        for h in range(nh):
            oa = mm(vs_s[h], es[h])
            ot_s[h * hdim : (h + 1) * hdim, at] = (oa[:hdim, :] * (1.0 / oa[hdim : hdim + 1, :])).astype(BF16)
        return 0

    lax.fori_loop(0, tokens // bq, block, 0, unroll=True)
    o_ref[...] = ot_s[...].T


def attend_fwd(qt, kt, vt, vrow, heads, hdim, slots, bq=BQ, nh=2):
    inner = heads * hdim
    w = nh * hdim
    seqs = qt.shape[1] // slots
    tcol = pl.BlockSpec((w, slots), lambda s, p: (p, s))
    return pl.pallas_call(
        functools.partial(attend_fwd_kernel, hdim, min(bq, slots), nh),
        grid=(seqs, heads // nh),
        in_specs=[tcol, tcol, tcol, pl.BlockSpec((1, 1, slots), lambda s, p: (s, 0, 0))],
        out_specs=pl.BlockSpec((slots, w), lambda s, p: (s, p)),
        out_shape=jax.ShapeDtypeStruct((seqs * slots, inner), BF16),
        scratch_shapes=[pltpu.VMEM((w, slots), BF16), pltpu.VMEM((nh, slots, hdim), BF16), pltpu.VMEM((nh, hdim + 16, slots), BF16)],
        compiler_params=pltpu.CompilerParams(vmem_limit_bytes=VMEM),
        cost_estimate=cost(16),
        name="attend_fwd",
    )(qt, kt, vt, vrow)


def out_rows_kernel(inner, cuts, steps, image_ref, x_ref, dz_ref, lng_ref, w_ref, wa_ref, wb_ref, o_ref, hid_ref, of_ref, *refs):
    pieces = len(cuts) - 1
    near, far = refs[:pieces], refs[pieces : 2 * pieces]
    out_ref, din_ref, both, sem = refs[-4:]
    tm = x_ref.shape[0]
    now = pl.program_id(0)

    @pl.when(now == 0)
    def _():
        for step in range(steps):
            for k, at, low, n in overlaps(cuts, step, tm):
                for side, parts in enumerate((near, far)):
                    pltpu.make_async_copy(parts[k].at[pl.ds(at, n)], both.at[step, side, pl.ds(low, n)], sem.at[step]).start()

    x = x_ref[...].astype(F32)
    centre = x - jnp.mean(x, axis=-1, keepdims=True)
    r = lax.rsqrt(jnp.mean(centre * centre, axis=-1, keepdims=True) + EPS)
    n = centre * r
    scaled = n * lng_ref[...]
    xn = scaled.astype(BF16)
    hidden = wb_ref.shape[1] // 2
    total = mm(o_ref[...], w_ref[:inner, :]) + mm(hid_ref[...], w_ref[inner:, :]) + mm(of_ref[...], wa_ref[...], NT)
    parts = []
    for c in range(0, hidden, 512):
        parts.append(gelu_parts(mm(xn, wb_ref[:, c : c + 512]))[0].astype(BF16))
    total = total + mm(jnp.concatenate(parts, axis=1), wb_ref[:, hidden:], NT)
    out_ref[...] = (x + total).astype(BF16)
    pltpu.make_async_copy(both.at[now], both.at[now], sem.at[now]).wait()
    a = (both[now, 0] + both[now, 1]) * lng_ref[...]
    back = r * (a - jnp.mean(a, axis=-1, keepdims=True) - n * jnp.mean(a * n, axis=-1, keepdims=True))
    din_ref[...] = (dz_ref[...].astype(F32) + back).astype(BF16)


def out_rows(image, x, dz, lng, wout, wa, wb, o, right, of, near, far, cuts, prior, tm=256):
    slots, inner = o.shape
    go, width = wout.shape
    steps = slots // tm
    row = lambda n: pl.BlockSpec((tm, n), lambda i, im: (i, 0))
    of_image = lambda n: pl.BlockSpec((tm, n), lambda i, im: (im[0] * steps + i, 0))
    at = of_image(width)
    whole = lambda a: pl.BlockSpec(a.shape, lambda i, im: (0,) * a.ndim, pipeline_mode=pl.Buffered(1))
    given = [image, x, dz, lng, wout, wa, wb, o, right, of, *near, *far]
    raw = pl.BlockSpec(memory_space=pl.ANY)
    return pl.pallas_call(
        functools.partial(out_rows_kernel, inner, cuts, steps),
        grid_spec=pltpu.PrefetchScalarGridSpec(
            num_scalar_prefetch=1,
            grid=(steps,),
            in_specs=[at, at, whole(lng), whole(wout), whole(wa), whole(wb), row(inner), of_image(go - inner), of_image(inner)] + [raw] * (len(near) + len(far) + 2),
            out_specs=[at, at],
            scratch_shapes=[pltpu.VMEM((steps, 2, tm, width), F32), pltpu.SemaphoreType.DMA((steps,))],
        ),
        out_shape=[jax.ShapeDtypeStruct(x.shape, BF16)] * 2,
        input_output_aliases={len(given) + k: k for k in range(2)},
        compiler_params=pltpu.CompilerParams(vmem_limit_bytes=VMEM),
        cost_estimate=cost(18),
        name="out_rows",
    )(*given, *prior)


def early_kernel(left_ref, right_ref, out_ref):
    out_ref[...] = mm(left_ref[...], right_ref[...])


def early_grads(left, right, tn=512):
    width, tokens = left.shape[0] // 2, left.shape[1]
    both = right.shape[1]
    steps = both // tn
    return pl.pallas_call(
        early_kernel,
        grid=(steps,),
        in_specs=[pl.BlockSpec((width, tokens), lambda j: (jnp.where(j < steps // 2, 0, 1), 0)), pl.BlockSpec((tokens, tn), lambda j: (0, j))],
        out_specs=pl.BlockSpec((width, tn), lambda j: (0, j)),
        out_shape=jax.ShapeDtypeStruct((width, both), F32),
        compiler_params=pltpu.CompilerParams(vmem_limit_bytes=VMEM),
        cost_estimate=cost(16),
        name="early_grads",
    )(left, right)


def late_kernel(seqs, low, core_ref, *refs):
    dzt, xnt = refs[:seqs], refs[seqs : 2 * seqs]
    o, dq, dk, dv = (refs[(2 + k) * seqs : (3 + k) * seqs] for k in range(4))
    small, keep, send = refs[-3:]
    width = o[0].shape[1]

    def store(cols, v):
        for half in range(2):
            rows = jnp.concatenate([v[b : b + low] for b in range(half * low, v.shape[0], 2 * low)], axis=0)

            @pl.when(core_ref[0] == half)
            def _():
                keep[:, cols] = rows

            @pl.when(core_ref[0] != half)
            def _():
                send[:, cols] = rows

    for k, (left, right) in enumerate(((dzt, o), (xnt, dq), (xnt, dk), (xnt, dv))):
        store(slice(k * width, (k + 1) * width), sum(mm(left[s][...], right[s][...]) for s in range(seqs)))
    store(slice(4 * width, 4 * width + 128), jnp.broadcast_to(small[...], (small.shape[0], 128)))


def late_grads(core, left, o, dq, dk, dv, small, low):
    seqs = len(o)
    slots, inner = o[0].shape
    width = left.shape[0] // 2
    tm = 4 * low
    while tm < 192:
        tm *= 2
    steps = width // tm
    above = [pl.BlockSpec((tm, slots), lambda i, c, s=s: (i, s)) for s in range(seqs)]
    below = [pl.BlockSpec((tm, slots), lambda i, c, s=s: (steps + i, s)) for s in range(seqs)]
    whole = pl.BlockSpec((slots, inner), lambda i, c: (0, 0), pipeline_mode=pl.Buffered(1))
    wide = 4 * inner + 128
    out = pl.BlockSpec((tm // 2, wide), lambda i, c: (i, 0))
    return pl.pallas_call(
        functools.partial(late_kernel, seqs, low),
        grid_spec=pltpu.PrefetchScalarGridSpec(
            num_scalar_prefetch=1,
            grid=(steps,),
            in_specs=above + below + [whole] * (4 * seqs) + [pl.BlockSpec((tm, 1), lambda i, c: (i, 0))],
            out_specs=[out, out],
        ),
        out_shape=[jax.ShapeDtypeStruct((width // 2, wide), F32)] * 2,
        compiler_params=pltpu.CompilerParams(vmem_limit_bytes=VMEM),
        cost_estimate=cost(12),
        name="late_grads",
    )(core, *[left] * (2 * seqs), *o, *dq, *dk, *dv, small)


def gate(value, *done):
    return lax.optimization_barrier((value, *done))[0]


def per_device(shards, patches, keep_mask, counts, ln_gain, w_in, q_gain, k_gain, w_out, d_out):
    seqs, slots, width = patches.shape
    heads, hdim = q_gain.shape
    inner = heads * hdim
    swap = [(0, 1), (1, 0)]
    scale = hdim ** (-0.5)
    win, wout = w_in[0], w_out[0]
    hidden = wout.shape[0] - inner
    x = patches.reshape(seqs * slots, width)
    dz = d_out.reshape(seqs * slots, width)
    slot_ids = jnp.arange(slots, dtype=jnp.int32)
    valid = (slot_ids[None, :] < counts[:, None]) & ((keep_mask == 1) | (slot_ids[None, :] == 0))
    vrow = valid.astype(F32).reshape(seqs, 1, slots)
    qg = q_gain.reshape(inner, 1)
    kg = k_gain.reshape(inner, 1)
    lng = ln_gain.reshape(1, width)
    qgs = qg * (scale * LOG2E)
    across = lambda v: lax.ppermute(v, "head", swap)

    def pair(v, bit):
        return lax.ppermute(v, "dp", [(i, i ^ bit) for i in range(shards)])

    number = [jnp.full((1,), s, jnp.int32) for s in range(seqs)]
    me = lax.axis_index("dp")

    quarter = width // 4

    def rows_of(bit, left_cols, right_rows):
        mine = ((me // bit) % 2) + 2 * (me % 2)
        rows = lax.dynamic_slice(win, (mine * quarter, left_cols[0]), (quarter, left_cols[1] - left_cols[0]))
        cols = lax.dynamic_slice(wout, (right_rows[0], mine * quarter), (right_rows[1] - right_rows[0], quarter))
        return mine.astype(jnp.int32).reshape(1), jnp.concatenate([rows.astype(F32), cols.astype(F32).T], axis=1)

    mine_a, piece_a = rows_of(2, (0, 3 * inner), (0, inner))
    mine_b, piece_b = rows_of(4, (3 * inner, win.shape[1]), (inner, wout.shape[0]))
    gains = across(jnp.concatenate([qgs, kg], axis=0).reshape(-1, 128))
    split = quarter * 7 // 12
    b = [[across(piece_b[:split])]]

    low = width // shards
    cell = lambda v, axis, at: lax.dynamic_index_in_dim(v, at, axis, False)
    others = shards // 4

    def by_two(v, w):
        bit = (me // 2) % 2
        v, w = (u.reshape(others, 2, low, -1) for u in (v, w))
        return cell(v, 1, bit) + cell(w, 1, bit), cell(v, 1, 1 - bit) + cell(w, 1, 1 - bit)

    def to_all(v, w):
        part = lambda m: cell(v, 0, (me // 4) ^ m) + cell(w, 0, (me // 4) ^ m)
        return part(0), [pair(part(m), 4 * m) for m in range(1, others)]

    def heads_of(s, first):
        return attend(number[s], first, kt, vt, dot, rq, rk, vrow, qg, kg, heads, hdim, slots)

    left, qt, kt, vt, dot, rq, rk, right = project(x, dz, lng, win, wout, qgs, kg, heads, hdim)
    o0, dq0, dk0, dv0, gq0, gk0 = heads_of(0, gate(qt, *b[0], gains))
    a = [across(gate(piece_a, *b[0]))]
    b.append([pair(b[0][0], 4)])
    cuts = (0, slots // 8, slots)
    n0 = back_rows(number[0], gate(dq0, *a), dk0, dv0, right, win, cuts)
    b[0].append(across(gate(piece_b[split:], *a)))
    a.append(pair(a[0], 2))
    f0 = [across(v) for v in n0]
    early = early_grads(gate(left, *n0), right)
    early = gate(early, b[0][1], b[1][0], a[1], f0[0])
    early_rs = lax.psum_scatter(early, "dp", scatter_dimension=0, tiled=True)
    b[1].append(pair(b[0][1], 4))
    o1, dq1, dk1, dv1, gq1, gk1 = heads_of(1, gate(qt, early))
    n1 = back_rows(number[1], gate(dq1, b[1][1]), dk1, dv1, right, win, (0, slots))
    a += [pair(gate(v, dq1), 1) for v in a]
    b += [[pair(gate(v, dq1), 1) for v in part] for part in b]
    part = lambda v: v.reshape(heads, shards, hdim // shards).transpose(1, 0, 2).reshape(shards, -1)
    small = jnp.concatenate([part(gq0 + gq1), part(gk0 + gk1)], axis=1)
    small = jnp.pad(small, ((0, 0), (0, low - small.shape[1]))).reshape(width, 1)
    core = (me % 2).astype(jnp.int32).reshape(1)
    keep, send = late_grads(core, gate(left, *n1), [o0, o1], [dq0, dq1], [dk0, dk1], [dv0, dv1], small, low)
    send = gate(send, *a, *b[2], *b[3], f0[1])
    f1 = [across(gate(v, send)) for v in n1]
    got = pair(send, 1)
    keep, send = by_two(keep, got)
    got = pair(send, 2)
    wb = unpack(mine_b, [(gate(b[0][0], send), b[0][1])] + b[1:])
    gains = gains.reshape(-1, 1)
    qf, kf, vf, wa, *blank = heads_fwd(mine_a, gate(gains[:inner], wb), gains[inner:], left, a, heads, hdim)
    of = attend_fwd(qf, kf, vf, vrow, heads, hdim, slots)
    keep, got = to_all(keep, gate(got, of))
    outs = out_rows(number[0], gate(x, keep), dz, lng, wout, wa, wb, o0, right, of, n0, f0, cuts, blank)
    late_rs = keep + sum(got)
    g_w_out = jnp.concatenate([late_rs[:, :inner], early_rs[:, :hidden]], axis=1).T[None]
    g_w_in = jnp.concatenate([late_rs[:, inner : 4 * inner], early_rs[:, hidden:]], axis=1)[None]
    band = lambda v: lax.dynamic_slice_in_dim(v, me * (width // shards), width // shards, 0)
    g_ln = jnp.sum(band(win).astype(F32) * g_w_in[0], axis=1) / band(ln_gain)
    bo, d_in = out_rows(number[1], gate(x, outs[0], *f1), dz, lng, wout, wa, wb, o1, right, of, n1, f1, (0, slots), outs)
    block_output = bo.reshape(patches.shape)
    d_in = d_in.reshape(patches.shape)
    g_ln = g_ln + across(g_ln)
    terms = late_rs[:, 4 * inner]
    count = inner // shards
    g_q = terms[:count].reshape(heads, hdim // shards)
    g_k = terms[count : 2 * count].reshape(heads, hdim // shards)
    return block_output, d_in, g_ln, g_w_in, g_q, g_k, g_w_out


def solution(mesh):
    placed = (
        P("dp", None, None),
        P("dp", None),
        P("dp"),
        P(),
        P("head", None, None),
        P("head", None),
        P("head", None),
        P("head", None, None),
        P("dp", None, None),
    )
    return jax.shard_map(
        functools.partial(per_device, mesh.shape["dp"]),
        mesh=mesh,
        in_specs=placed,
        out_specs=(
            P("dp", None, None),
            P("dp", None, None),
            P("dp"),
            P("head", "dp", None),
            P("head", "dp"),
            P("head", "dp"),
            P("head", None, "dp"),
        ),
        check_vma=False,
    )
```
